512 devices in a mesh: axial: 32 (over x, z), azim: 8 (over y), bank: 2 (over core).
Axes of the slice: x: 4, y: 8, z: 8, core: 2. Of those that a mesh axis runs over, the one named last changes fastest.
Arguments:
- adjoint_state: float32 [2, 64, 256, 2048], P('bank', None, 'axial', 'azim'), may hold values from -6 to 6
- adjoint_source: float32 [2, 64, 256, 2048], P('bank', None, 'axial', 'azim'), may hold values from -6 to 6
- reaction_rate: float32 [2, 256, 2048], P('bank', 'axial', 'azim'), may hold values from 0.5 to 2
- jacobian: float32 [2, 64, 64], P('bank'), may hold values from -0.75 to 0.75
- lifting: float32 [2, 6, 256, 2048], P('bank', None, 'axial', 'azim'), may hold values from -0.125 to 0.125
- separator: int32 [32, 8, 2, 6], P('axial', 'azim', 'bank'), may hold values from 0 to 2047
- leaf_schur: float32 [32, 8, 2, 384, 384], P('axial', 'azim', 'bank'), may hold values from -14 to 43, as said below
Outputs:
- interface_adjoint: float32 [32, 8, 2, 384], P('axial', 'azim', 'bank')
The draws below stay inside these ranges and needn't reach their ends.
Inputs may be any that keep to these rules, and one draw needn't show every extreme that they name: `separator`: a cell k = row * 256 + column of the device's own block. `leaf_schur`: every leaf block is symmetric positive definite.
All inputs are finite; a program needn't handle non-finite values.
Results may differ from the reference program's by a relative error of at most 0.0003.
Values sent between devices are 32-bit elements; how exact they have to be, the bound alone decides.
A program may use at most 64 MiB of HBM per device.

```python
import math
import jax
import jax.numpy as jnp
from jax import lax

NVAR = 64
SEP = 6
CX = 8
CZ = 256
W = 384
NAX = 256
NAZ = 2048
N_AXIAL = 32
N_AZIM = 8
N_BANK = 2


def draw_leaf_schur(key, part):
    key_rate, key_shift = jax.random.split(key)
    full_shape = (N_AXIAL, N_AZIM, N_BANK, W, W)
    rows = lax.broadcasted_iota(jnp.int32, (W, W), 0)
    cols = lax.broadcasted_iota(jnp.int32, (W, W), 1)
    distance = jnp.abs(rows - cols)
    kernel = jnp.ones((W, W), jnp.float32)
    for level in range(16):
        kernel = kernel * jnp.where(distance - 1 >= 1 << level, 0.25, 1.0).astype(jnp.float32)
    levels = jax.random.randint(key_rate, full_shape, 4, 13)
    shift = jnp.exp(jax.random.uniform(key_shift, full_shape[:-1], jnp.float32, jnp.log(0.01), jnp.log(0.08)))
    rates = levels.astype(jnp.float32) * 0.125
    rates = jnp.where(rows < cols, rates, jnp.swapaxes(rates, -1, -2))
    offdiag = jnp.where(distance > 0, rates * kernel, 0.0)
    row_total = jnp.sum(offdiag, axis=-1)
    diagonal = row_total + shift
    return 8.0 * jnp.where(distance == 0, diagonal[..., None], -offdiag)


def place_ends(entries, rng, smallest, largest):
    extent = entries.shape
    spot = [jax.random.randint(jax.random.fold_in(rng, axis), (), 0, extent[axis]) for axis in range(len(extent))]
    entries = entries.at[tuple(spot)].set(smallest)
    longest = extent.index(max(extent))
    spot[longest] = (spot[longest] + 1) % extent[longest]
    return entries.at[tuple(spot)].set(largest)


def shard_levels(rng, dims, cuts, least, largest):
    def one(dim, blocks):
        steps = jax.random.uniform(jax.random.fold_in(jax.random.fold_in(rng, 6), dim), (blocks,), jnp.float32, least / len(cuts), largest / len(cuts))
        return jnp.repeat(jnp.exp(steps), dims[dim] // blocks).reshape((-1,) + (1,) * (len(dims) - dim - 1))

    factor_of = one(*cuts[0])
    for cut in cuts[1:]:
        factor_of = factor_of * one(*cut)
    return factor_of


def centred(rng, dims, scale, reach, pieces=(), dtype=jnp.bfloat16):
    gain = shard_levels(rng, dims, pieces, -0.22, 0.18) if pieces else 1.0
    drawn = jax.random.normal(rng, dims, jnp.float32) * scale * gain
    return jnp.minimum(jnp.maximum(drawn, -reach), reach).astype(dtype)


def setup_inputs(seed: int = 0) -> dict:
    keys = jax.random.split(jax.random.key(seed), 8)
    return {
        "adjoint_state": centred(keys[0], (N_BANK, NVAR, NAX, NAZ), 1.0, 6.0, ((0, 2), (2, 32), (3, 8)), jnp.float32),
        "adjoint_source": centred(keys[1], (N_BANK, NVAR, NAX, NAZ), 1.0, 6.0, ((0, 2), (2, 32), (3, 8)), jnp.float32),
        "reaction_rate": jnp.clip(jnp.exp(math.log(2.0) - 1.3862944 * jax.random.uniform(keys[2], (N_BANK, NAX, NAZ), jnp.float32) ** shard_levels(keys[2], (N_BANK, NAX, NAZ), ((0, 2), (1, 32), (2, 8)), -0.2, 0.2)), 0.5, 2.0),
        "jacobian": centred(keys[3], (N_BANK, NVAR, NVAR), NVAR ** -0.5, 0.75, ((0, 2),), jnp.float32),
        "lifting": centred(keys[4], (N_BANK, SEP, NAX, NAZ), (CX * CZ) ** -0.5, 0.125, ((0, 2), (2, 32), (3, 8)), jnp.float32),
        "separator": place_ends(jax.random.randint(keys[5], (N_AXIAL, N_AZIM, N_BANK, SEP), 0, CX * CZ), jax.random.fold_in(keys[5], 1), 0, (CX * CZ) - 1).astype(jnp.int32),
        "leaf_schur": draw_leaf_schur(jax.random.fold_in(keys[7], 71), 0),
    }


highest = lax.Precision.HIGHEST
diffusion = 0.5

def residual_field(adjoint_state, adjoint_source, reaction_rate, jacobian):
    scaled = reaction_rate[:, None] * adjoint_state
    reaction = jnp.einsum('bvu,bvxz->buxz', jacobian, scaled, precision=highest)
    padded = jnp.pad(adjoint_state, ((0, 0), (0, 0), (1, 1), (0, 0)))
    neighbours = padded[:, :, 2:, :] + padded[:, :, :-2, :]
    neighbours = neighbours + jnp.roll(adjoint_state, 1, axis=3) + jnp.roll(adjoint_state, -1, axis=3)
    return adjoint_source - reaction - diffusion * (4.0 * adjoint_state - neighbours)

def to_blocks(values):
    chans = values.shape[1]
    shaped = values.reshape(N_BANK, chans, N_AXIAL, CX, N_AZIM, CZ)
    shaped = jnp.transpose(shaped, (2, 4, 0, 1, 3, 5))
    return shaped.reshape(N_AXIAL, N_AZIM, N_BANK, chans, CX * CZ)

def eliminate(first_shared, second_shared, shared_rhs, middle):
    shared_sum = first_shared[:, middle:] + second_shared[:, middle:]
    factor = jnp.linalg.cholesky(shared_sum)
    coupling = jnp.concatenate([first_shared[:, :middle], second_shared[:, :middle]], axis=1)
    inner = jax.scipy.linalg.solve_triangular(factor, coupling, lower=True)
    coupled = jax.scipy.linalg.solve_triangular(factor, inner, lower=True, trans=1)
    inner_rhs = jax.scipy.linalg.solve_triangular(factor, shared_rhs, lower=True)
    shifted = jax.scipy.linalg.solve_triangular(factor, inner_rhs, lower=True, trans=1)
    return (coupled, shifted)

def merge_pair(first_schur, second_schur, first_rhs, second_rhs):
    middle = first_schur.shape[0] // 2
    coupled, shifted = eliminate(first_schur[middle:], second_schur[middle:], first_rhs[middle:] + second_rhs[middle:], middle)
    zero_block = jnp.zeros((middle, middle), jnp.float32)
    upper_rows = jnp.concatenate([first_schur[:middle, :middle], zero_block], axis=1) - jnp.dot(first_schur[:middle, middle:], coupled, precision=highest)
    lower_rows = jnp.concatenate([zero_block, second_schur[:middle, :middle]], axis=1) - jnp.dot(second_schur[:middle, middle:], coupled, precision=highest)
    upper_rhs = first_rhs[:middle] - jnp.dot(first_schur[:middle, middle:], shifted, precision=highest)
    lower_rhs = second_rhs[:middle] - jnp.dot(second_schur[:middle, middle:], shifted, precision=highest)
    parent = jnp.concatenate([upper_rows, lower_rows], axis=0)
    parent_rhs = jnp.concatenate([upper_rhs, lower_rhs])
    return (parent, parent_rhs, coupled, shifted)

def reference(adjoint_state, adjoint_source, reaction_rate, jacobian, lifting, separator, leaf_schur):
    residual = residual_field(adjoint_state, adjoint_source, reaction_rate, jacobian)
    residual_blocks = to_blocks(residual)
    lifting_blocks = to_blocks(lifting)
    picked = jnp.take_along_axis(residual_blocks, separator[:, :, :, None, :].astype(jnp.int32), axis=4)
    picked = jnp.swapaxes(picked, 3, 4)
    lifted = jnp.einsum('azbck,azbvk->azbcv', lifting_blocks, residual_blocks, precision=highest)
    width = SEP * NVAR
    middle = width // 2
    rhs = (picked + lifted).reshape(-1, width)
    schur = leaf_schur.reshape(-1, width, width)
    saved_levels = []
    while schur.shape[0] > 1:
        paired = schur.reshape(-1, 2, width, width)
        paired_rhs = rhs.reshape(-1, 2, width)
        schur, rhs, coupled, shifted = jax.vmap(merge_pair)(paired[:, 0], paired[:, 1], paired_rhs[:, 0], paired_rhs[:, 1])
        saved_levels.append((coupled, shifted))
    root_factor = jnp.linalg.cholesky(schur[0])
    inner = jax.scipy.linalg.solve_triangular(root_factor, rhs[0], lower=True)
    answer = jax.scipy.linalg.solve_triangular(root_factor, inner, lower=True, trans=1)[None, :]
    for coupled, shifted in reversed(saved_levels):
        separator_values = shifted - jnp.einsum('phw,pw->ph', coupled, answer, precision=highest)
        first_child = jnp.concatenate([answer[:, :middle], separator_values], axis=1)
        second_child = jnp.concatenate([answer[:, middle:], separator_values], axis=1)
        answer = jnp.stack([first_child, second_child], axis=1).reshape(-1, width)
    return answer.reshape(N_AXIAL, N_AZIM, N_BANK, width)
```

```python
import functools

import jax
import jax.numpy as jnp
from jax import lax
from jax.experimental import pallas as pl
from jax.experimental.pallas import tpu as pltpu
from jax.sharding import PartitionSpec as P

highest = lax.Precision.HIGHEST
diffusion = 0.5
F32 = jnp.float32
MESH = pl.DeviceIdType.MESH
H = 192
A = 128
B = 64


def extended(array, sides, width, wrap):
    for axis, dim in sides:
        size, length = (lax.axis_size(axis), array.shape[dim])
        up = [(i, (i + 1) % size) for i in range(size if wrap else size - 1)]
        down = [(j, i) for i, j in up]
        last = lax.slice_in_dim(array, length - width, length, axis=dim)
        first = lax.slice_in_dim(array, 0, width, axis=dim)
        before = lax.ppermute(last, axis, up)
        after = lax.ppermute(first, axis, down)
        array = jnp.concatenate([before, array, after], axis=dim)
    return array


def mm(a, b):
    return lax.dot_general(a, b, (((1,), (0,)), ((), ())), precision=highest, preferred_element_type=F32)


def mtn(a, b):
    return lax.dot_general(a, b, (((0,), (0,)), ((), ())), precision=highest, preferred_element_type=F32)


def mnt(a, b):
    return lax.dot_general(a, b, (((1,), (1,)), ((), ())), precision=highest, preferred_element_type=F32)


def row_of(x, i):
    return jnp.broadcast_to(x[i : i + 1, :], x.shape)


def col_of(x, i):
    return jnp.broadcast_to(x[:, i : i + 1], x.shape)


def tree_sum(terms):
    terms = list(terms)
    while len(terms) > 1:
        terms = [terms[i] + terms[i + 1] if i + 1 < len(terms) else terms[i] for i in range(0, len(terms), 2)]
    return terms[0]


def invert8(columns):
    sub = lax.broadcasted_iota(jnp.int32, (8, 128), 0)
    columns = list(columns)
    for p in range(0, 8, 2):
        x, y = columns[p], columns[p + 1]
        a, b, c = row_of(x, p), row_of(y, p), row_of(y, p + 1)
        scale = 1.0 / (a * c - b * b)
        first, second = sub == p, sub == p + 1
        pivot_rows = jnp.logical_or(first, second)
        hu = jnp.where(first, c, jnp.where(second, -b, y * b - x * c))
        hv = jnp.where(first, -b, jnp.where(second, a, x * b - y * a))
        for j in range(8):
            if j in (p, p + 1):
                continue
            u, v = row_of(columns[j], p), row_of(columns[j], p + 1)
            columns[j] = jnp.where(pivot_rows, 0.0, columns[j]) + (hu * u + hv * v) * scale
        columns[p] = hu * scale
        columns[p + 1] = hv * scale
    return columns


def gauss_jordan(tiles, n):
    count, parts = len(tiles), len(tiles[0])
    sub = lax.broadcasted_iota(jnp.int32, (8, 128), 0)
    lane = lax.broadcasted_iota(jnp.int32, (8, 128), 1)
    for k in range(n // 8):
        part, start = (8 * k) // 128, (8 * k) % 128
        block = jnp.logical_and(lane >= start, lane < start + 8)
        inverse = invert8([col_of(tiles[k][part], start + j) for j in range(8)])
        pivot = []
        for l in range(parts):
            value = tiles[k][l]
            if l == part:
                value = jnp.where(block, jnp.where(lane - start == sub, 1.0, 0.0), value)
            pivot.append(tree_sum([inverse[j] * row_of(value, j) for j in range(8)]))
        rows = [[row_of(pivot[l], j) for j in range(8)] for l in range(parts)]
        for i in [i % count for i in range(k + 1, k + count)]:
            factors = [col_of(tiles[i][part], start + j) for j in range(8)]
            fresh = []
            for l in range(parts):
                base = tiles[i][l]
                if l == part:
                    base = jnp.where(block, 0.0, base)
                fresh.append(base - tree_sum([factors[j] * rows[l][j] for j in range(8)]))
            tiles[i] = fresh
        tiles[k] = pivot
    return tiles


def tree_kernel(
    sizes, leaf_ref, rhs_ref, out_ref, ssb, eb, oob, fb, ainv, yb, sc, xs, zs, xv, up_send, up_recv, down_send, down_recv
):
    n_axial, n_azim, n_bank = sizes
    total = n_axial * n_azim * n_bank
    merges = total.bit_length() - 1
    me = (lax.axis_index("axial") * n_azim + lax.axis_index("azim")) * n_bank + lax.axis_index("bank")

    def device(n):
        return (n // (n_azim * n_bank), (n // n_bank) % n_azim, n % n_bank)

    def step_of(level):
        if isinstance(level, int):
            return 1 << (level if level < merges else merges - 1)
        step = jnp.int32(1)
        for l in range(1, merges + 1):
            step = jnp.where(level == l, jnp.int32(1 << (l if l < merges else merges - 1)), step)
        return step

    def receives(level):
        return jnp.logical_and(level != merges - 1, me % (2 * step_of(level)) == 0)

    def sends(level):
        step = step_of(level)
        return jnp.logical_and(level != merges - 1, me % (2 * step) == step)

    def computes(level):
        return jnp.where(level == merges - 1, me % step_of(level) == 0, me % (2 * step_of(level)) == 0)

    pieces = (ssb, eb, oob, fb)

    def upward(level, which):
        ref = pieces[which]
        return pltpu.make_async_remote_copy(
            src_ref=ref.at[level, 0],
            dst_ref=ref.at[level, 1],
            send_sem=up_send.at[which],
            recv_sem=up_recv.at[level, which],
            device_id=device(me - step_of(level)),
            device_id_type=MESH,
        )

    def downward(level, peer):
        return pltpu.make_async_remote_copy(
            src_ref=xv.at[level, 1],
            dst_ref=xv.at[level, 0],
            send_sem=down_send.at[level],
            recv_sem=down_recv.at[level],
            device_id=device(peer),
            device_id_type=MESH,
        )

    barrier = pltpu.get_barrier_semaphore()
    levels = [l for l in range(merges + 1) if l != merges - 1]
    for level in levels:
        step = step_of(level)

        @pl.when(me % step == 0)
        def _():
            peer = jnp.where(me % (2 * step) == 0, me + step, me - step)
            pl.semaphore_signal(barrier, inc=1, device_id=device(peer), device_id_type=MESH)

    def put_ss(level, value):
        ssb[level, 0, :, 0:A] = value[0:A, 0:A]
        ssb[level, 0, 0:B, A : 2 * A] = jnp.concatenate([value[0:B, A:H], value[A:H, A:H]], axis=1)
        ssb[level, 0, B:A, A : 2 * A] = jnp.concatenate([value[B:A, A:H], jnp.zeros((A - B, B), F32)], axis=1)

    put_ss(0, leaf_ref[H:, H:])
    eb[0, 0] = leaf_ref[H:, :H]
    oob[0, 0] = leaf_ref[:H, :H]
    fb[0, 0, 0] = jnp.broadcast_to(rhs_ref[:, :H], (8, H))
    fb[0, 0, 1] = jnp.broadcast_to(rhs_ref[:, H:], (8, H))
    local = merges - 1
    ssb[local, 1] = jnp.zeros((A, 2 * A), F32)
    eb[local, 1] = jnp.zeros((H, H), F32)
    oob[local, 1] = jnp.zeros((H, H), F32)
    fb[local, 1] = jnp.zeros((2, 8, H), F32)
    sc[...] = jnp.zeros((B, 2 * B), F32)

    peers = jnp.int32(0)
    for level in levels:
        peers = peers + jnp.where(me % step_of(level) == 0, 1, 0)
    pl.semaphore_wait(barrier, peers)

    @pl.when(sends(0))
    def _():
        for which in range(4):
            upward(0, which).start()

    def ascend(level, carry):
        @pl.when(computes(level))
        def _():
            first = jnp.where(level >= merges - 2, jnp.where(level == merges, 0, 1), 0)
            second = 1 - first

            @pl.when(level != local)
            def _():
                upward(level, 0).wait_recv()

            tiles = []
            for i in range(A // 8):
                tiles.append(
                    [
                        ssb[level, 0, 8 * i : 8 * i + 8, 128 * l : 128 * l + 128]
                        + ssb[level, 1, 8 * i : 8 * i + 8, 128 * l : 128 * l + 128]
                        for l in range(2)
                    ]
                )
            tiles = gauss_jordan(tiles, A)
            for i in range(A // 8):
                ainv[8 * i : 8 * i + 8, :] = tiles[i][0]
                yb[8 * i : 8 * i + 8, :] = tiles[i][1][:, 0:B]

            @pl.when(level != local)
            def _():
                for which in range(1, 4):
                    upward(level, which).wait_recv()

            y = yb[...]
            bc = ssb[level, 0, :, A : 2 * A] + ssb[level, 1, :, A : 2 * A]
            corner = bc[0:B, B : 2 * B] - mtn(bc[:, 0:B], y)
            sc[:, 0:B] = corner
            low = [[sc[8 * i : 8 * i + 8, :]] for i in range(B // 8)]
            low = gauss_jordan(low, B)
            e = [eb[level, first], eb[level, second]]
            inverse_a = ainv[...]
            g = [mm(inverse_a, e[q][0:A]) for q in range(2)]
            t = [e[q][A:H] - mtn(y, e[q][0:A]) for q in range(2)]
            for i in range(B // 8):
                sc[8 * i : 8 * i + 8, :] = low[i][0]
            inverse_s = sc[:, 0:B]
            x2 = [mm(inverse_s, t[q]) for q in range(2)]
            ss = oob[level, second] - mtn(e[1][0:A], g[1]) - mtn(t[1], x2[1])
            put_ss(level + 1, ss)

            @pl.when(jnp.logical_and(level < merges, sends(level + 1)))
            def _():
                upward(level + 1, 0).start()

            eb[level + 1, 0] = -mtn(e[1][0:A], g[0]) - mtn(t[1], x2[0])
            oob[level + 1, 0] = oob[level, first] - mtn(e[0][0:A], g[0]) - mtn(t[0], x2[0])
            for q in range(2):
                xs[level, q, 0:A] = g[q] - mm(y, x2[q])
                xs[level, q, A:H] = x2[q]
            shared = fb[level, 0, 1] + fb[level, 1, 1]
            tail = shared[:, A:H] - mm(shared[:, 0:A], y)
            z2 = mm(tail, inverse_s)
            z1 = mm(shared[:, 0:A], inverse_a) - mnt(z2, y)
            zs[level, :, 0:A] = z1
            zs[level, :, A:H] = z2
            for q, slot in ((0, first), (1, second)):
                fb[level + 1, 0, q] = fb[level, slot, 0] - mm(z1, e[q][0:A]) - mm(z2, e[q][A:H])

            @pl.when(jnp.logical_and(level < merges, sends(level + 1)))
            def _():
                for which in range(1, 4):
                    upward(level + 1, which).start()

        return carry

    lax.fori_loop(0, merges + 1, ascend, 0)

    xv[merges + 1, 0] = jnp.zeros((2, 8, H), F32)

    def descend(i, carry):
        level = merges - i

        @pl.when(sends(level))
        def _():
            for which in range(4):
                upward(level, which).wait_send()
            downward(level, me).wait_recv()

        @pl.when(computes(level))
        def _():
            above = level + 1
            first = jnp.where(level >= merges - 2, jnp.where(level == merges, 0, 1), 0)
            y = zs[level] - mnt(xv[above, 0, 0], xs[level, 0]) - mnt(xv[above, 0, 1], xs[level, 1])
            xv[level, 0, 0] = xv[above, 0, first]
            xv[level, 0, 1] = y
            xv[level, 1, 0] = xv[above, 0, 1 - first]
            xv[level, 1, 1] = y

            @pl.when(level != local)
            def _():
                downward(level, me + step_of(level)).start()

        return carry

    lax.fori_loop(0, merges + 1, descend, 0)
    out_ref[:, 0:H] = xv[0, 0, 0, 0:1]
    out_ref[:, H:] = xv[0, 0, 1, 0:1]

    def finish(level, carry):
        @pl.when(receives(level))
        def _():
            downward(level, me + step_of(level)).wait_send()

        return carry

    lax.fori_loop(0, merges + 1, finish, 0)


def solve_tree(schur, rhs, sizes):
    total = sizes[0] * sizes[1] * sizes[2]
    slots = total.bit_length() + 1
    vmem = pl.BlockSpec(memory_space=pltpu.VMEM)
    return pl.pallas_call(
        functools.partial(tree_kernel, sizes),
        out_shape=jax.ShapeDtypeStruct((1, 2 * H), F32),
        in_specs=[vmem, vmem],
        out_specs=vmem,
        scratch_shapes=[
            pltpu.VMEM((slots, 2, A, 2 * A), F32),
            pltpu.VMEM((slots, 2, H, H), F32),
            pltpu.VMEM((slots, 2, H, H), F32),
            pltpu.VMEM((slots, 2, 2, 8, H), F32),
            pltpu.VMEM((A, A), F32),
            pltpu.VMEM((A, B), F32),
            pltpu.VMEM((B, 2 * B), F32),
            pltpu.VMEM((slots, 2, H, H), F32),
            pltpu.VMEM((slots, 8, H), F32),
            pltpu.VMEM((slots, 2, 2, 8, H), F32),
            pltpu.SemaphoreType.DMA((4,)),
            pltpu.SemaphoreType.DMA((slots, 4)),
            pltpu.SemaphoreType.DMA((slots,)),
            pltpu.SemaphoreType.DMA((slots,)),
        ],
        compiler_params=pltpu.CompilerParams(
            collective_id=0, has_side_effects=True, vmem_limit_bytes=48 * 1024 * 1024
        ),
    )(schur, rhs)


def leaf_rhs(adjoint_state, adjoint_source, reaction_rate, jacobian, lifting, separator):
    along_axial = extended(adjoint_state, (("axial", 2),), 1, False)
    along_azim = extended(adjoint_state, (("azim", 3),), 1, True)
    scaled = reaction_rate[:, None] * adjoint_state
    reaction = jnp.einsum("bvu,bvxz->buxz", jacobian, scaled, precision=highest)
    neighbours = along_axial[:, :, 2:, :] + along_axial[:, :, :-2, :]
    neighbours = neighbours + along_azim[:, :, :, :-2] + along_azim[:, :, :, 2:]
    residual = adjoint_source - reaction - diffusion * (4.0 * adjoint_state - neighbours)
    chans = residual.shape[1]
    flat_residual = residual.reshape(chans, -1)
    sep_cells = separator.reshape(-1)
    picked = jnp.take(flat_residual, sep_cells, axis=1).T
    lifted = jnp.einsum(
        "ck,vk->cv", lifting.reshape(sep_cells.shape[0], -1), flat_residual, precision=highest
    )
    return (picked + lifted).reshape(1, -1)


def body(sizes, adjoint_state, adjoint_source, reaction_rate, jacobian, lifting, separator, leaf_schur):
    rhs = leaf_rhs(adjoint_state, adjoint_source, reaction_rate, jacobian, lifting, separator)
    answer = solve_tree(leaf_schur.reshape(2 * H, 2 * H), rhs, sizes)
    return answer.reshape(1, 1, 1, 2 * H)


def solution(mesh):
    sizes = (mesh.shape["axial"], mesh.shape["azim"], mesh.shape["bank"])
    in_specs = (
        P("bank", None, "axial", "azim"),
        P("bank", None, "axial", "azim"),
        P("bank", "axial", "azim"),
        P("bank", None, None),
        P("bank", None, "axial", "azim"),
        P("axial", "azim", "bank", None),
        P("axial", "azim", "bank", None, None),
    )
    out_specs = P("axial", "azim", "bank", None)
    return jax.shard_map(
        functools.partial(body, sizes), mesh=mesh, in_specs=in_specs, out_specs=out_specs, check_vma=False
    )
```

```python
import functools

import jax
import jax.numpy as jnp
from jax import lax
from jax.experimental import pallas as pl
from jax.experimental.pallas import tpu as pltpu
from jax.sharding import PartitionSpec as P

highest = lax.Precision.HIGHEST
diffusion = 0.5
F32 = jnp.float32
BF16 = jnp.bfloat16
MESH = pl.DeviceIdType.MESH
H = 192
B = 64
W = 256


def mm(a, b):
    return lax.dot_general(a, b, (((1,), (0,)), ((), ())), precision=highest, preferred_element_type=F32)


def mtn(a, b):
    return lax.dot_general(a, b, (((0,), (0,)), ((), ())), precision=highest, preferred_element_type=F32)


def mnt(a, b):
    return lax.dot_general(a, b, (((1,), (1,)), ((), ())), precision=highest, preferred_element_type=F32)


def mnt_narrow(a, b):
    return lax.dot_general(a, b, (((1,), (1,)), ((), ())), preferred_element_type=F32)


def halves(x):
    high = x.astype(BF16)
    return high, (x - high.astype(F32)).astype(BF16)


def row_of(x, i):
    return jnp.broadcast_to(x[i : i + 1, :], x.shape)


def col_of(x, i):
    return jnp.broadcast_to(x[:, i : i + 1], x.shape)


def tree_sum(terms):
    terms = list(terms)
    while len(terms) > 1:
        terms = [terms[i] + terms[i + 1] if i + 1 < len(terms) else terms[i] for i in range(0, len(terms), 2)]
    return terms[0]


def invert8(columns):
    sub = lax.broadcasted_iota(jnp.int32, (8, 128), 0)
    columns = list(columns)
    for p in range(0, 8, 2):
        x, y = columns[p], columns[p + 1]
        a, b, c = row_of(x, p), row_of(y, p), row_of(y, p + 1)
        scale = 1.0 / (a * c - b * b)
        first, second = sub == p, sub == p + 1
        pivot_rows = jnp.logical_or(first, second)
        hu = jnp.where(first, c, jnp.where(second, -b, y * b - x * c))
        hv = jnp.where(first, -b, jnp.where(second, a, x * b - y * a))
        for j in range(8):
            if j in (p, p + 1):
                continue
            u, v = row_of(columns[j], p), row_of(columns[j], p + 1)
            columns[j] = jnp.where(pivot_rows, 0.0, columns[j]) + (hu * u + hv * v) * scale
        columns[p] = hu * scale
        columns[p + 1] = hv * scale
    return columns


def gauss_jordan(tiles, offset):
    count, parts = len(tiles), len(tiles[0])
    sub = lax.broadcasted_iota(jnp.int32, (8, 128), 0)
    lane = lax.broadcasted_iota(jnp.int32, (8, 128), 1)
    for k in range(count):
        start = offset + 8 * k
        block = jnp.logical_and(lane >= start, lane < start + 8)
        inverse = invert8([col_of(tiles[k][0], start + j) for j in range(8)])
        pivot = []
        for l in range(parts):
            value = tiles[k][l]
            if l == 0:
                value = jnp.where(block, jnp.where(lane - start == sub, 1.0, 0.0), value)
            pivot.append(tree_sum([inverse[j] * row_of(value, j) for j in range(8)]))
        rows = [[row_of(pivot[l], j) for j in range(8)] for l in range(parts)]
        for i in [i % count for i in range(k + 1, k + count)]:
            factors = [col_of(tiles[i][0], start + j) for j in range(8)]
            fresh = []
            for l in range(parts):
                base = tiles[i][l]
                if l == 0:
                    base = jnp.where(block, 0.0, base)
                fresh.append(base - tree_sum([factors[j] * rows[l][j] for j in range(8)]))
            tiles[i] = fresh
        tiles[k] = pivot
    return tiles


def packed(m):
    return [
        m[0:B, 0:128],
        jnp.concatenate([m[0:B, 128:H], m[128:H, 128:H]], axis=1),
        jnp.concatenate([m[B:128, 128:H], m[B:128, B:128]], axis=1),
    ]


def tree_kernel(
    sizes, state, source, rate, jac, lift, sep, leaf, out_ref,
    psb, eb, oob, one, two, three, tt, gg, xh, xl, xv, xout, edge_rows, halo_rows, edge_cols, halo_cols,
    up_send, up_recv, halo_send, halo_recv, down_send, down_recv,
):
    n_axial, n_azim, n_bank = sizes
    total = n_axial * n_azim * n_bank
    merges = total.bit_length() - 1
    local = merges - 1
    i_axial, i_azim, i_bank = lax.axis_index("axial"), lax.axis_index("azim"), lax.axis_index("bank")
    me = (i_axial * n_azim + i_azim) * n_bank + i_bank
    channels, rows_here, cells = state.shape

    def device(n):
        return (n // (n_azim * n_bank), (n // n_bank) % n_azim, n % n_bank)

    def field(level):
        bit = level if level < local else merges - 1
        azim_top = (n_bank * n_azim).bit_length() - 2
        if n_azim == 8 and bit == azim_top:
            return bit - 2, 3
        if n_axial == 32 and bit == azim_top + 3:
            return bit - 2, 3
        if n_axial == 32 and bit == azim_top + 5:
            return bit - 1, 2
        return bit, 1

    exchanges = [l for l in range(merges + 1) if l != local]

    def partner_at(level):
        low, width = field(level)
        value = (me // (1 << low)) % (1 << width)
        return me + ((1 << width) - 1 - 2 * value) * (1 << low)

    def partner(level):
        if isinstance(level, int):
            return partner_at(level)
        n = partner_at(0)
        for l in exchanges[1:]:
            n = jnp.where(level == l, partner_at(l), n)
        return n

    def first_slot(level):
        slot = jnp.int32(0)
        for l in range(merges + 1):
            bit = (me // (1 << l)) % 2
            here = 1 if l == local else (0 if l == merges else (1 - bit if l == merges - 2 else bit))
            slot = jnp.where(level == l, here, slot)
        return slot

    def piece(which, level, slot):
        if which == 0:
            return psb.at[level, slot, :, 0:256]
        if which == 1:
            return psb.at[level, slot, :, 256:384]
        return (eb if which == 2 else oob).at[level, slot]

    def upward(level, which):
        return pltpu.make_async_remote_copy(
            src_ref=piece(which, level, 0),
            dst_ref=piece(which, level, 1),
            send_sem=up_send.at[level, which],
            recv_sem=up_recv.at[level, which],
            device_id=device(partner(level)),
            device_id_type=MESH,
        )

    def downward():
        return pltpu.make_async_remote_copy(
            src_ref=xout.at[0],
            dst_ref=xout.at[1],
            send_sem=down_send,
            recv_sem=down_recv,
            device_id=device(partner_at(0)),
            device_id_type=MESH,
        )

    left = (i_axial, lax.rem(i_azim + n_azim - 1, n_azim), i_bank)
    right = (i_axial, lax.rem(i_azim + 1, n_azim), i_bank)
    above = (i_axial - 1, i_azim, i_bank)
    below = (i_axial + 1, i_azim, i_bank)
    has_above, has_below = i_axial > 0, i_axial < n_axial - 1

    def halo(which):
        src, dst, to = (
            (edge_rows.at[0], halo_rows.at[1], above),
            (edge_rows.at[1], halo_rows.at[0], below),
            (edge_cols.at[0], halo_cols.at[1], left),
            (edge_cols.at[1], halo_cols.at[0], right),
        )[which]
        return pltpu.make_async_remote_copy(
            src_ref=src,
            dst_ref=dst,
            send_sem=halo_send.at[which],
            recv_sem=halo_recv.at[which],
            device_id=to,
            device_id_type=MESH,
        )

    halo_rows[...] = jnp.zeros_like(halo_rows)
    barrier = pltpu.get_barrier_semaphore()

    def greet(to):
        pl.semaphore_signal(barrier, inc=1, device_id=to, device_id_type=MESH)

    greet(left)
    greet(right)
    greet(device(partner_at(0)))
    pl.when(has_above)(lambda: greet(above))
    pl.when(has_below)(lambda: greet(below))

    @pl.when(i_bank == 0)
    def _():
        for level in exchanges[1:]:
            greet(device(partner_at(level)))

    lane128 = lax.broadcasted_iota(jnp.int32, (channels, 128), 1)
    edge_rows[0] = state[:, 0, :]
    edge_rows[1] = state[:, rows_here - 1, :]
    first_cols = jnp.zeros((channels, 128), F32)
    last_cols = jnp.zeros((channels, 128), F32)
    for r in range(rows_here):
        head, tail = state[:, r, 0:128], state[:, r, cells - 128 : cells]
        first_cols = jnp.where(lane128 == r, pltpu.roll(head, r, 1) if r else head, first_cols)
        last_cols = jnp.where(lane128 == r, pltpu.roll(tail, r + 1, 1), last_cols)
    edge_cols[0] = first_cols
    edge_cols[1] = last_cols

    def put(ref, level, parts):
        for l in range(3):
            ref[level, 0, :, 128 * l : 128 * l + 128] = parts[l]

    put(psb, 0, packed(leaf[H:, H:]))
    put(oob, 0, packed(leaf[:H, :H]))
    eb[0, 0, :, 0:H] = leaf[H:, :H]
    eb[0, 0, :, H:W] = jnp.zeros((H, W - H), F32)
    psb[local, 1] = jnp.zeros((B, 2 * H), F32)
    oob[local, 1] = jnp.zeros((B, 2 * H), F32)
    eb[local, 1] = jnp.zeros((H, W), F32)
    three[...] = jnp.zeros((B, 2 * B), F32)

    friends = 3 + jnp.where(has_above, 1, 0) + jnp.where(has_below, 1, 0)
    friends = friends + jnp.where(i_bank == 0, len(exchanges) - 1, 0)
    pl.semaphore_wait(barrier, friends)

    @pl.when(i_bank == 1)
    def _():
        for which in (0, 1, 3):
            upward(0, which).start()

    pl.when(has_above)(lambda: halo(0).start())
    pl.when(has_below)(lambda: halo(1).start())
    halo(2).start()
    halo(3).start()

    def front():
        pl.when(has_below)(lambda: halo(0).wait_recv())
        pl.when(has_above)(lambda: halo(1).wait_recv())
        halo(2).wait_recv()
        halo(3).wait_recv()
        lane = lax.broadcasted_iota(jnp.int32, (channels, cells), 1)
        lane6 = lax.broadcasted_iota(jnp.int32, (sep.shape[0], cells), 1)
        jacobian = jac[...]
        rhs = jnp.zeros((channels, sep.shape[0]), F32)
        for r in range(rows_here):
            here = state[:, r, :]
            up = state[:, r - 1, :] if r else halo_rows[0]
            down = state[:, r + 1, :] if r < rows_here - 1 else halo_rows[1]
            before = jnp.where(lane == 0, halo_cols[0][:, r : r + 1], pltpu.roll(here, 1, 1))
            after = jnp.where(lane == cells - 1, halo_cols[1][:, r : r + 1], pltpu.roll(here, cells - 1, 1))
            reaction = mtn(jacobian, rate[r : r + 1, :] * here)
            residual = source[:, r, :] - reaction - diffusion * (4.0 * here - (up + down + before + after))
            picks = jnp.where(lane6 + r * cells == sep[...], 1.0, 0.0)
            rhs = rhs + mnt(residual, picks + lift[:, r, :])
        for c in range(3):
            eb[0, 0, c * channels : (c + 1) * channels, H : H + 1] = rhs[:, c + 3 : c + 4]
            eb[0, 0, c * channels : (c + 1) * channels, H + 1 : H + 2] = rhs[:, c : c + 1]

    @pl.when(i_bank == 1)
    def _():
        front()
        upward(0, 2).start()

    def ascend(level, carry):
        @pl.when(level != local)
        def _():
            upward(level, 0).wait_recv()

        first = first_slot(level)
        second = 1 - first

        def both(i, l):
            rows, lanes = pl.ds(8 * i, 8), pl.ds(128 * l, 128)
            return psb[level, 0, rows, lanes] + psb[level, 1, rows, lanes]

        tiles = gauss_jordan([[both(i, 0), both(i, 1)] for i in range(8)], 0)
        for i in range(8):
            for l in range(2):
                one[8 * i : 8 * i + 8, 128 * l : 128 * l + 128] = tiles[i][l]

        @pl.when(level != local)
        def _():
            upward(level, 1).wait_recv()

        lane = lax.broadcasted_iota(jnp.int32, (B, 128), 1)
        head = psb[level, 0, :, 0:256] + psb[level, 1, :, 0:256]
        k12, k13, k33 = head[:, B:128], head[:, 128:H], head[:, H:]
        update = mtn(k12, one[...])
        two[...] = (
            psb[level, 0, :, 256:384] + psb[level, 1, :, 256:384] - jnp.where(lane < B, update[:, 128:], update[:, :128])
        )
        s23 = two[:, 0:B]
        tiles = gauss_jordan([[two[8 * i : 8 * i + 8, :]] for i in range(8)], B)
        corner = k33 - mtn(k13, one[:, 128:H])
        for i in range(8):
            two[8 * i : 8 * i + 8, :] = tiles[i][0]
        three[:, 0:B] = corner - mtn(s23, two[:, 0:B])

        pl.when(level == 0)(front)

        @pl.when(level != local)
        def _():
            upward(level, 2).wait_recv()

        @pl.when(jnp.logical_and(level != local, level != merges))
        def _():
            upward(level, 3).wait_recv()

        lane = lax.broadcasted_iota(jnp.int32, (H, W), 1)
        e = [eb[level, first], eb[level, second]]
        f = e[0] + e[1]
        outer_f = [e[0][:, 128:W], e[1][:, 128:W]]
        e[0] = jnp.where(lane < H, e[0], jnp.where(lane == H, f, 0.0))
        for q in range(2):
            m1 = mtn(one[:, 0:H], e[q][0:B])
            t2 = e[q][B:128] - m1[B:128]
            m2 = mtn(two[...], t2)
            tt[q, 0:B] = e[q][0:B]
            tt[q, B:128] = t2
            tt[q, 128:H] = e[q][128:H] - m1[128:H] - m2[0:B]
            gg[q, 0:B] = m1[0:B]
            gg[q, B:128] = m2[B:128]
        low = gauss_jordan([[three[8 * i : 8 * i + 8, :]] for i in range(8)], 0)
        before = packed(mtn(tt[1, 0:128, 0:H], gg[1, 0:128, 0:H]))
        for i in range(8):
            three[8 * i : 8 * i + 8, :] = low[i][0]
        gg[1, 128:H] = mm(three[:, 0:B], tt[1, 128:H])
        after = packed(mtn(tt[1, 128:H, 0:H], gg[1, 128:H, 0:H]))
        for l in range(3):
            lanes = pl.ds(128 * l, 128)
            psb[level + 1, 0, :, lanes] = oob[level, second, :, lanes] - before[l] - after[l]

        send = jnp.logical_and(level < merges, level + 1 != local)

        @pl.when(send)
        def _():
            upward(level + 1, 0).start()
            upward(level + 1, 1).start()

        gg[0, 128:H] = mm(three[:, 0:B], tt[0, 128:H])
        lane = lax.broadcasted_iota(jnp.int32, (H, 128), 1)
        cross = mtn(tt[1, :, 0:H], gg[0])
        outer = mtn(tt[0, :, 0:H], gg[0])
        eb[level + 1, 0, :, 0:128] = -cross[:, 0:128]
        shared_f = pltpu.roll(outer_f[1], 127, 1) - cross[:, 128:W]
        outer_f = outer_f[0] - pltpu.roll(outer[:, 128:W], 1, 1)
        eb[level + 1, 0, :, 128:W] = jnp.where(
            lane < B, -cross[:, 128:W], jnp.where(lane == B, shared_f, jnp.where(lane == B + 1, outer_f, 0.0))
        )

        @pl.when(send)
        def _():
            upward(level + 1, 2).start()

        parts = packed(outer)
        for l in range(3):
            lanes = pl.ds(128 * l, 128)
            oob[level + 1, 0, :, lanes] = oob[level, first, :, lanes] - parts[l]

        @pl.when(jnp.logical_and(send, level + 1 != merges))
        def _():
            upward(level + 1, 3).start()

        y12, y13, y23 = one[:, B:128], one[:, 128:H], two[:, 0:B]
        for q in range(2):
            x3 = gg[q, 128:H]
            x2 = gg[q, B:128] - mm(y23, x3)
            x1 = gg[q, 0:B] - mm(y12, x2) - mm(y13, x3)
            for r, x in enumerate((x1, x2, x3)):
                high, low = halves(x)
                xh[level, q, B * r : B * r + B] = high
                xl[level, q, B * r : B * r + B] = low
        return carry

    lane8 = lax.broadcasted_iota(jnp.int32, (8, W), 1)

    def descend(i, carry):
        level = merges - i
        first = first_slot(level)
        y = jnp.zeros((8, H), F32)
        for q in range(2):
            x = jnp.where(lane8 < H, -xv[level + 1, q], jnp.where(lane8 == H, 1.0 - q, 0.0))
            high, low = halves(x)
            y = y + (mnt_narrow(high, xh[level, q]) + (mnt_narrow(low, xh[level, q]) + mnt_narrow(high, xl[level, q])))
        xv[level, 0] = xv[level + 1, first]
        xv[level, 1, :, 0:H] = y
        return carry

    def wait_up(level, carry):
        @pl.when(level != local)
        def _():
            for which in range(3):
                upward(level, which).wait_send()

        @pl.when(jnp.logical_and(level != local, level != merges))
        def _():
            upward(level, 3).wait_send()

        return carry

    @pl.when(i_bank == 0)
    def _():
        lax.fori_loop(0, merges + 1, ascend, 0)
        xv[...] = jnp.zeros_like(xv)
        lax.fori_loop(0, merges + 1, descend, 0)
        xout[0, 0] = xv[1, 1 - first_slot(0)]
        xout[0, 1] = xv[0, 1]
        downward().start()
        out_ref[:, 0:H] = xv[0, 0, 0:1, 0:H]
        out_ref[:, H:] = xv[0, 1, 0:1, 0:H]
        lax.fori_loop(1, merges + 1, wait_up, 0)
        downward().wait_send()

    @pl.when(i_bank == 1)
    def _():
        for which in range(4):
            upward(0, which).wait_send()
        downward().wait_recv()
        out_ref[:, 0:H] = xout[1, 0, 0:1, 0:H]
        out_ref[:, H:] = xout[1, 1, 0:1, 0:H]

    pl.when(has_above)(lambda: halo(0).wait_send())
    pl.when(has_below)(lambda: halo(1).wait_send())
    halo(2).wait_send()
    halo(3).wait_send()


def solve_tree(sizes, state, source, rate, jac, lift, sep, leaf):
    total = sizes[0] * sizes[1] * sizes[2]
    slots = total.bit_length() + 1
    channels, rows, cells = state.shape
    vmem = pl.BlockSpec(memory_space=pltpu.VMEM)
    return pl.pallas_call(
        functools.partial(tree_kernel, sizes),
        out_shape=jax.ShapeDtypeStruct((1, 2 * H), F32),
        in_specs=[vmem] * 7,
        out_specs=vmem,
        scratch_shapes=[
            pltpu.VMEM((slots, 2, B, 2 * H), F32),
            pltpu.VMEM((slots, 2, H, W), F32),
            pltpu.VMEM((slots, 2, B, 2 * H), F32),
            pltpu.VMEM((B, 256), F32),
            pltpu.VMEM((B, 128), F32),
            pltpu.VMEM((B, 128), F32),
            pltpu.VMEM((2, H, W), F32),
            pltpu.VMEM((2, H, W), F32),
            pltpu.VMEM((slots, 2, H, W), BF16),
            pltpu.VMEM((slots, 2, H, W), BF16),
            pltpu.VMEM((slots, 2, 8, W), F32),
            pltpu.VMEM((2, 2, 8, W), F32),
            pltpu.VMEM((2, channels, cells), F32),
            pltpu.VMEM((2, channels, cells), F32),
            pltpu.VMEM((2, channels, 128), F32),
            pltpu.VMEM((2, channels, 128), F32),
            pltpu.SemaphoreType.DMA((slots, 4)),
            pltpu.SemaphoreType.DMA((slots, 4)),
            pltpu.SemaphoreType.DMA((4,)),
            pltpu.SemaphoreType.DMA((4,)),
            pltpu.SemaphoreType.DMA,
            pltpu.SemaphoreType.DMA,
        ],
        compiler_params=pltpu.CompilerParams(
            collective_id=0, has_side_effects=True, vmem_limit_bytes=48 * 1024 * 1024
        ),
    )(state, source, rate, jac, lift, sep, leaf)


def body(sizes, adjoint_state, adjoint_source, reaction_rate, jacobian, lifting, separator, leaf_schur):
    answer = solve_tree(
        sizes,
        adjoint_state[0],
        adjoint_source[0],
        reaction_rate[0],
        jacobian[0],
        lifting[0],
        separator.reshape(-1, 1),
        leaf_schur.reshape(2 * H, 2 * H),
    )
    return answer.reshape(1, 1, 1, 2 * H)


def solution(mesh):
    sizes = (mesh.shape["axial"], mesh.shape["azim"], mesh.shape["bank"])
    in_specs = (
        P("bank", None, "axial", "azim"),
        P("bank", None, "axial", "azim"),
        P("bank", "axial", "azim"),
        P("bank", None, None),
        P("bank", None, "axial", "azim"),
        P("axial", "azim", "bank", None),
        P("axial", "azim", "bank", None, None),
    )
    out_specs = P("axial", "azim", "bank", None)
    return jax.shard_map(
        functools.partial(body, sizes), mesh=mesh, in_specs=in_specs, out_specs=out_specs, check_vma=False
    )
```

```python
import functools

import jax
import jax.numpy as jnp
from jax import lax
from jax.experimental import pallas as pl
from jax.experimental.pallas import tpu as pltpu
from jax.sharding import PartitionSpec as P

highest = lax.Precision.HIGHEST
diffusion = 0.5
F32 = jnp.float32
BF16 = jnp.bfloat16
MESH = pl.DeviceIdType.MESH
H = 192
B = 64
W = 256


def mm(a, b):
    return lax.dot_general(a, b, (((1,), (0,)), ((), ())), precision=highest, preferred_element_type=F32)


def mtn(a, b):
    return lax.dot_general(a, b, (((0,), (0,)), ((), ())), precision=highest, preferred_element_type=F32)


def mnt(a, b):
    return lax.dot_general(a, b, (((1,), (1,)), ((), ())), precision=highest, preferred_element_type=F32)


def mnt_narrow(a, b):
    return lax.dot_general(a, b, (((1,), (1,)), ((), ())), preferred_element_type=F32)


def halves(x):
    high = x.astype(BF16)
    return high, (x - high.astype(F32)).astype(BF16)


def row_of(x, i):
    return jnp.broadcast_to(x[i : i + 1, :], x.shape)


def col_of(x, i):
    return jnp.broadcast_to(x[:, i : i + 1], x.shape)


def tree_sum(terms):
    terms = list(terms)
    while len(terms) > 1:
        terms = [terms[i] + terms[i + 1] if i + 1 < len(terms) else terms[i] for i in range(0, len(terms), 2)]
    return terms[0]


def invert8(columns):
    sub = lax.broadcasted_iota(jnp.int32, (8, 128), 0)
    columns = list(columns)
    for p in range(0, 8, 2):
        x, y = columns[p], columns[p + 1]
        a, b, c = row_of(x, p), row_of(y, p), row_of(y, p + 1)
        scale = 1.0 / (a * c - b * b)
        first, second = sub == p, sub == p + 1
        pivot_rows = jnp.logical_or(first, second)
        hu = jnp.where(first, c, jnp.where(second, -b, y * b - x * c))
        hv = jnp.where(first, -b, jnp.where(second, a, x * b - y * a))
        for j in range(8):
            if j in (p, p + 1):
                continue
            u, v = row_of(columns[j], p), row_of(columns[j], p + 1)
            columns[j] = jnp.where(pivot_rows, 0.0, columns[j]) + (hu * u + hv * v) * scale
        columns[p] = hu * scale
        columns[p + 1] = hv * scale
    return columns


def gauss_jordan(tiles, offset):
    count, parts = len(tiles), len(tiles[0])
    sub = lax.broadcasted_iota(jnp.int32, (8, 128), 0)
    lane = lax.broadcasted_iota(jnp.int32, (8, 128), 1)
    for k in range(count):
        start = offset + 8 * k
        block = jnp.logical_and(lane >= start, lane < start + 8)
        inverse = invert8([col_of(tiles[k][0], start + j) for j in range(8)])
        pivot = []
        for l in range(parts):
            value = tiles[k][l]
            if l == 0:
                value = jnp.where(block, jnp.where(lane - start == sub, 1.0, 0.0), value)
            pivot.append(tree_sum([inverse[j] * row_of(value, j) for j in range(8)]))
        rows = [[row_of(pivot[l], j) for j in range(8)] for l in range(parts)]
        for i in [i % count for i in range(k + 1, k + count)]:
            factors = [col_of(tiles[i][0], start + j) for j in range(8)]
            fresh = []
            for l in range(parts):
                base = tiles[i][l]
                if l == 0:
                    base = jnp.where(block, 0.0, base)
                fresh.append(base - tree_sum([factors[j] * rows[l][j] for j in range(8)]))
            tiles[i] = fresh
        tiles[k] = pivot
    return tiles


def packed(m):
    return [
        m[0:B, 0:128],
        jnp.concatenate([m[0:B, 128:H], m[128:H, 128:H]], axis=1),
        jnp.concatenate([m[B:128, 128:H], m[B:128, B:128]], axis=1),
    ]


def tree_kernel(
    sizes, state_in, source_in, rate_in, jac_in, lift_in, sep, leaf_in, out_ref,
    state, source, rate, jac, lift, leaf, in_sem,
    psb, eb, oob, one, two, three, tt, gg, xh, xl, xv, xout, edge_rows, halo_rows, edge_cols, halo_cols,
    up_send, up_recv, halo_send, halo_recv, down_send, down_recv,
):
    n_axial, n_azim, n_bank = sizes
    total = n_axial * n_azim * n_bank
    merges = total.bit_length() - 1
    local = merges - 1
    i_axial, i_azim, i_bank = lax.axis_index("axial"), lax.axis_index("azim"), lax.axis_index("bank")
    me = (i_axial * n_azim + i_azim) * n_bank + i_bank
    channels, rows_here, cells = state.shape

    def device(n):
        return (n // (n_azim * n_bank), (n // n_bank) % n_azim, n % n_bank)

    def field(level):
        bit = level if level < local else merges - 1
        azim_top = (n_bank * n_azim).bit_length() - 2
        if n_azim == 8 and bit == azim_top:
            return bit - 2, 3
        if n_axial == 32 and bit == azim_top + 3:
            return bit - 2, 3
        if n_axial == 32 and bit == azim_top + 5:
            return bit - 1, 2
        return bit, 1

    exchanges = [l for l in range(merges + 1) if l != local]

    def partner_at(level):
        low, width = field(level)
        value = (me // (1 << low)) % (1 << width)
        return me + ((1 << width) - 1 - 2 * value) * (1 << low)

    def partner(level):
        if isinstance(level, int):
            return partner_at(level)
        n = partner_at(0)
        for l in exchanges[1:]:
            n = jnp.where(level == l, partner_at(l), n)
        return n

    def first_slot(level):
        slot = jnp.int32(0)
        for l in range(merges + 1):
            bit = (me // (1 << l)) % 2
            here = 1 if l == local else (0 if l == merges else (1 - bit if l == merges - 2 else bit))
            slot = jnp.where(level == l, here, slot)
        return slot

    def piece(which, level, slot):
        if which == 0:
            return psb.at[level, slot, :, 0:256]
        if which == 1:
            return psb.at[level, slot, :, 256:384]
        return (eb if which == 2 else oob).at[level, slot]

    def upward(level, which):
        return pltpu.make_async_remote_copy(
            src_ref=piece(which, level, 0),
            dst_ref=piece(which, level, 1),
            send_sem=up_send.at[level, which],
            recv_sem=up_recv.at[level, which],
            device_id=device(partner(level)),
            device_id_type=MESH,
        )

    def downward():
        return pltpu.make_async_remote_copy(
            src_ref=xout.at[0],
            dst_ref=xout.at[1],
            send_sem=down_send,
            recv_sem=down_recv,
            device_id=device(partner_at(0)),
            device_id_type=MESH,
        )

    left = (i_axial, lax.rem(i_azim + n_azim - 1, n_azim), i_bank)
    right = (i_axial, lax.rem(i_azim + 1, n_azim), i_bank)
    above = (i_axial - 1, i_azim, i_bank)
    below = (i_axial + 1, i_azim, i_bank)
    has_above, has_below = i_axial > 0, i_axial < n_axial - 1

    def halo(which):
        src, dst, to = (
            (edge_rows.at[0], halo_rows.at[1], above),
            (edge_rows.at[1], halo_rows.at[0], below),
            (edge_cols.at[0], halo_cols.at[1], left),
            (edge_cols.at[1], halo_cols.at[0], right),
        )[which]
        return pltpu.make_async_remote_copy(
            src_ref=src,
            dst_ref=dst,
            send_sem=halo_send.at[which],
            recv_sem=halo_recv.at[which],
            device_id=to,
            device_id_type=MESH,
        )

    loads = [
        pltpu.make_async_copy(src, dst, in_sem.at[i])
        for i, (src, dst) in enumerate(
            ((leaf_in, leaf), (state_in, state), (source_in, source), (lift_in, lift), (rate_in, rate), (jac_in, jac))
        )
    ]
    for load in loads:
        load.start()
    halo_rows[...] = jnp.zeros_like(halo_rows)
    barrier = pltpu.get_barrier_semaphore()

    def greet(to):
        pl.semaphore_signal(barrier, inc=1, device_id=to, device_id_type=MESH)

    greet(left)
    greet(right)
    greet(device(partner_at(0)))
    pl.when(has_above)(lambda: greet(above))
    pl.when(has_below)(lambda: greet(below))

    @pl.when(i_bank == 0)
    def _():
        for level in exchanges[1:]:
            greet(device(partner_at(level)))

    loads[1].wait()
    lane128 = lax.broadcasted_iota(jnp.int32, (channels, 128), 1)
    edge_rows[0] = state[:, 0, :]
    edge_rows[1] = state[:, rows_here - 1, :]
    first_cols = jnp.zeros((channels, 128), F32)
    last_cols = jnp.zeros((channels, 128), F32)
    for r in range(rows_here):
        head, tail = state[:, r, 0:128], state[:, r, cells - 128 : cells]
        first_cols = jnp.where(lane128 == r, pltpu.roll(head, r, 1) if r else head, first_cols)
        last_cols = jnp.where(lane128 == r, pltpu.roll(tail, r + 1, 1), last_cols)
    edge_cols[0] = first_cols
    edge_cols[1] = last_cols

    def put(ref, level, parts):
        for l in range(3):
            ref[level, 0, :, 128 * l : 128 * l + 128] = parts[l]

    loads[0].wait()
    put(psb, 0, packed(leaf[H:, H:]))
    put(oob, 0, packed(leaf[:H, :H]))
    eb[0, 0, :, 0:H] = leaf[H:, :H]
    eb[0, 0, :, H:W] = jnp.zeros((H, W - H), F32)
    psb[local, 1] = jnp.zeros((B, 2 * H), F32)
    oob[local, 1] = jnp.zeros((B, 2 * H), F32)
    eb[local, 1] = jnp.zeros((H, W), F32)
    three[...] = jnp.zeros((B, 2 * B), F32)

    friends = 3 + jnp.where(has_above, 1, 0) + jnp.where(has_below, 1, 0)
    friends = friends + jnp.where(i_bank == 0, len(exchanges) - 1, 0)
    pl.semaphore_wait(barrier, friends)

    @pl.when(i_bank == 1)
    def _():
        for which in (0, 1, 3):
            upward(0, which).start()

    pl.when(has_above)(lambda: halo(0).start())
    pl.when(has_below)(lambda: halo(1).start())
    halo(2).start()
    halo(3).start()

    def front():
        pl.when(has_below)(lambda: halo(0).wait_recv())
        pl.when(has_above)(lambda: halo(1).wait_recv())
        halo(2).wait_recv()
        halo(3).wait_recv()
        for load in loads[2:]:
            load.wait()
        lane = lax.broadcasted_iota(jnp.int32, (channels, cells), 1)
        lane6 = lax.broadcasted_iota(jnp.int32, (sep.shape[0], cells), 1)
        jacobian = jac[...]
        rhs = jnp.zeros((channels, sep.shape[0]), F32)
        for r in range(rows_here):
            here = state[:, r, :]
            up = state[:, r - 1, :] if r else halo_rows[0]
            down = state[:, r + 1, :] if r < rows_here - 1 else halo_rows[1]
            before = jnp.where(lane == 0, halo_cols[0][:, r : r + 1], pltpu.roll(here, 1, 1))
            after = jnp.where(lane == cells - 1, halo_cols[1][:, r : r + 1], pltpu.roll(here, cells - 1, 1))
            reaction = mtn(jacobian, rate[r : r + 1, :] * here)
            residual = source[:, r, :] - reaction - diffusion * (4.0 * here - (up + down + before + after))
            picks = jnp.where(lane6 + r * cells == sep[...], 1.0, 0.0)
            rhs = rhs + mnt(residual, picks + lift[:, r, :])
        for c in range(3):
            eb[0, 0, c * channels : (c + 1) * channels, H : H + 1] = rhs[:, c + 3 : c + 4]
            eb[0, 0, c * channels : (c + 1) * channels, H + 1 : H + 2] = rhs[:, c : c + 1]

    @pl.when(i_bank == 1)
    def _():
        front()
        upward(0, 2).start()

    def ascend(level, carry):
        @pl.when(level != local)
        def _():
            upward(level, 0).wait_recv()

        first = first_slot(level)
        second = 1 - first

        def both(i, l):
            rows, lanes = pl.ds(8 * i, 8), pl.ds(128 * l, 128)
            return psb[level, 0, rows, lanes] + psb[level, 1, rows, lanes]

        tiles = gauss_jordan([[both(i, 0), both(i, 1)] for i in range(8)], 0)
        for i in range(8):
            for l in range(2):
                one[8 * i : 8 * i + 8, 128 * l : 128 * l + 128] = tiles[i][l]

        @pl.when(level != local)
        def _():
            upward(level, 1).wait_recv()

        lane = lax.broadcasted_iota(jnp.int32, (B, 128), 1)
        head = psb[level, 0, :, 0:256] + psb[level, 1, :, 0:256]
        k12, k13, k33 = head[:, B:128], head[:, 128:H], head[:, H:]
        update = mtn(k12, one[...])
        two[...] = (
            psb[level, 0, :, 256:384] + psb[level, 1, :, 256:384] - jnp.where(lane < B, update[:, 128:], update[:, :128])
        )
        s23 = two[:, 0:B]
        tiles = gauss_jordan([[two[8 * i : 8 * i + 8, :]] for i in range(8)], B)
        corner = k33 - mtn(k13, one[:, 128:H])
        for i in range(8):
            two[8 * i : 8 * i + 8, :] = tiles[i][0]
        three[:, 0:B] = corner - mtn(s23, two[:, 0:B])

        pl.when(level == 0)(front)

        @pl.when(level != local)
        def _():
            upward(level, 2).wait_recv()

        lane = lax.broadcasted_iota(jnp.int32, (H, 128), 1)
        e_first, e_second = eb[level, first], eb[level, second]
        tail_first, tail_second = e_first[:, 128:W], e_second[:, 128:W]
        outer_f = [tail_first, tail_second]
        tail_first = jnp.where(lane == B, tail_first + tail_second, jnp.where(lane < B, tail_first, 0.0))
        e = jnp.concatenate([e_second, e_first[:, 0:128], tail_first], axis=1)
        m1 = mtn(one[:, 0:H], e[0:B])
        t2 = e[B:128] - m1[B:128]
        m2 = mtn(two[...], t2)
        tt[0:B] = e[0:B]
        tt[B:128] = t2
        tt[128:H] = e[128:H] - m1[128:H] - m2[0:B]
        gg[0:B] = m1[0:B]
        gg[B:128] = m2[B:128]
        low = gauss_jordan([[three[8 * i : 8 * i + 8, :]] for i in range(8)], 0)
        for i in range(8):
            three[8 * i : 8 * i + 8, :] = low[i][0]

        @pl.when(jnp.logical_and(level != local, level != merges))
        def _():
            upward(level, 3).wait_recv()

        gg[128:H] = mm(three[:, 0:B], tt[128:H])
        parts = packed(mtn(tt[:, 0:H], gg[:, 0:H]))
        for l in range(3):
            lanes = pl.ds(128 * l, 128)
            psb[level + 1, 0, :, lanes] = oob[level, second, :, lanes] - parts[l]

        send = jnp.logical_and(level < merges, level + 1 != local)

        @pl.when(send)
        def _():
            upward(level + 1, 0).start()
            upward(level + 1, 1).start()

        cross = mtn(tt[:, 0:H], gg[:, W:])
        eb[level + 1, 0, :, 0:128] = -cross[:, 0:128]
        outer = mtn(tt[:, W : W + H], gg[:, W:])
        shared_f = pltpu.roll(outer_f[1], 127, 1) - cross[:, 128:W]
        outer_f = outer_f[0] - pltpu.roll(outer[:, 128:W], 1, 1)
        eb[level + 1, 0, :, 128:W] = jnp.where(
            lane < B, -cross[:, 128:W], jnp.where(lane == B, shared_f, jnp.where(lane == B + 1, outer_f, 0.0))
        )

        @pl.when(send)
        def _():
            upward(level + 1, 2).start()

        parts = packed(outer)
        for l in range(3):
            lanes = pl.ds(128 * l, 128)
            oob[level + 1, 0, :, lanes] = oob[level, first, :, lanes] - parts[l]

        @pl.when(jnp.logical_and(send, level + 1 != merges))
        def _():
            upward(level + 1, 3).start()

        x3 = gg[128:H]
        x2 = gg[B:128] - mm(two[:, 0:B], x3)
        x1 = gg[0:B] - mm(one[:, B:128], x2) - mm(one[:, 128:H], x3)
        for r, x in enumerate((x1, x2, x3)):
            high, low = halves(x)
            xh[level, B * r : B * r + B] = high
            xl[level, B * r : B * r + B] = low
        return carry

    lane8 = lax.broadcasted_iota(jnp.int32, (8, W), 1)

    def descend(i, carry):
        level = merges - i
        first = first_slot(level)
        x = [jnp.where(lane8 < H, -xv[level + 1, q], jnp.where(lane8 == H, 1.0 - q, 0.0)) for q in (1, 0)]
        high, low = halves(jnp.concatenate(x, axis=1))
        y = mnt_narrow(high, xh[level]) + (mnt_narrow(low, xh[level]) + mnt_narrow(high, xl[level]))
        xv[level, 0] = xv[level + 1, first]
        xv[level, 1, :, 0:H] = y
        return carry

    def wait_up(level, carry):
        @pl.when(level != local)
        def _():
            for which in range(3):
                upward(level, which).wait_send()

        @pl.when(jnp.logical_and(level != local, level != merges))
        def _():
            upward(level, 3).wait_send()

        return carry

    @pl.when(i_bank == 0)
    def _():
        lax.fori_loop(0, merges + 1, ascend, 0)
        xv[...] = jnp.zeros_like(xv)
        lax.fori_loop(0, merges + 1, descend, 0)
        xout[0, 0] = xv[1, 1 - first_slot(0)]
        xout[0, 1] = xv[0, 1]
        downward().start()
        out_ref[:, 0:H] = xv[0, 0, 0:1, 0:H]
        out_ref[:, H:] = xv[0, 1, 0:1, 0:H]
        lax.fori_loop(1, merges + 1, wait_up, 0)
        downward().wait_send()

    @pl.when(i_bank == 1)
    def _():
        for which in range(4):
            upward(0, which).wait_send()
        downward().wait_recv()
        out_ref[:, 0:H] = xout[1, 0, 0:1, 0:H]
        out_ref[:, H:] = xout[1, 1, 0:1, 0:H]

    pl.when(has_above)(lambda: halo(0).wait_send())
    pl.when(has_below)(lambda: halo(1).wait_send())
    halo(2).wait_send()
    halo(3).wait_send()


def solve_tree(sizes, state, source, rate, jac, lift, sep, leaf):
    total = sizes[0] * sizes[1] * sizes[2]
    slots = total.bit_length() + 1
    channels, rows, cells = state.shape
    vmem, hbm = pl.BlockSpec(memory_space=pltpu.VMEM), pl.BlockSpec(memory_space=pl.ANY)
    return pl.pallas_call(
        functools.partial(tree_kernel, sizes),
        out_shape=jax.ShapeDtypeStruct((1, 2 * H), F32),
        in_specs=[hbm] * 5 + [vmem, hbm],
        out_specs=vmem,
        scratch_shapes=[
            *(pltpu.VMEM(x.shape, F32) for x in (state, source, rate, jac, lift, leaf)),
            pltpu.SemaphoreType.DMA((6,)),
            pltpu.VMEM((slots, 2, B, 2 * H), F32),
            pltpu.VMEM((slots, 2, H, W), F32),
            pltpu.VMEM((slots, 2, B, 2 * H), F32),
            pltpu.VMEM((B, 256), F32),
            pltpu.VMEM((B, 128), F32),
            pltpu.VMEM((B, 128), F32),
            pltpu.VMEM((H, 2 * W), F32),
            pltpu.VMEM((H, 2 * W), F32),
            pltpu.VMEM((slots, H, 2 * W), BF16),
            pltpu.VMEM((slots, H, 2 * W), BF16),
            pltpu.VMEM((slots, 2, 8, W), F32),
            pltpu.VMEM((2, 2, 8, W), F32),
            pltpu.VMEM((2, channels, cells), F32),
            pltpu.VMEM((2, channels, cells), F32),
            pltpu.VMEM((2, channels, 128), F32),
            pltpu.VMEM((2, channels, 128), F32),
            pltpu.SemaphoreType.DMA((slots, 4)),
            pltpu.SemaphoreType.DMA((slots, 4)),
            pltpu.SemaphoreType.DMA((4,)),
            pltpu.SemaphoreType.DMA((4,)),
            pltpu.SemaphoreType.DMA,
            pltpu.SemaphoreType.DMA,
        ],
        compiler_params=pltpu.CompilerParams(
            collective_id=0, has_side_effects=True, vmem_limit_bytes=48 * 1024 * 1024
        ),
    )(state, source, rate, jac, lift, sep, leaf)


def body(sizes, adjoint_state, adjoint_source, reaction_rate, jacobian, lifting, separator, leaf_schur):
    answer = solve_tree(
        sizes,
        adjoint_state[0],
        adjoint_source[0],
        reaction_rate[0],
        jacobian[0],
        lifting[0],
        separator.reshape(-1, 1),
        leaf_schur.reshape(2 * H, 2 * H),
    )
    return answer.reshape(1, 1, 1, 2 * H)


def solution(mesh):
    sizes = (mesh.shape["axial"], mesh.shape["azim"], mesh.shape["bank"])
    in_specs = (
        P("bank", None, "axial", "azim"),
        P("bank", None, "axial", "azim"),
        P("bank", "axial", "azim"),
        P("bank", None, None),
        P("bank", None, "axial", "azim"),
        P("axial", "azim", "bank", None),
        P("axial", "azim", "bank", None, None),
    )
    out_specs = P("axial", "azim", "bank", None)
    return jax.shard_map(
        functools.partial(body, sizes), mesh=mesh, in_specs=in_specs, out_specs=out_specs, check_vma=False
    )
```

```python
import functools

import jax
import jax.numpy as jnp
from jax import lax
from jax.experimental import pallas as pl
from jax.experimental.pallas import tpu as pltpu
from jax.sharding import PartitionSpec as P

highest = lax.Precision.HIGH
diffusion = 0.5
F32 = jnp.float32
BF16 = jnp.bfloat16
MESH = pl.DeviceIdType.MESH
H = 192
B = 64
W = 256


def mm(a, b):
    return lax.dot_general(a, b, (((1,), (0,)), ((), ())), precision=highest, preferred_element_type=F32)


def mtn(a, b):
    return lax.dot_general(a, b, (((0,), (0,)), ((), ())), precision=highest, preferred_element_type=F32)


def mnt(a, b):
    return lax.dot_general(a, b, (((1,), (1,)), ((), ())), precision=highest, preferred_element_type=F32)


def mnt_narrow(a, b):
    return lax.dot_general(a, b, (((1,), (1,)), ((), ())), preferred_element_type=F32)


def halves(x):
    high = x.astype(BF16)
    return high, (x - high.astype(F32)).astype(BF16)


def row_of(x, i):
    return jnp.broadcast_to(x[i : i + 1, :], x.shape)


def col_of(x, i):
    return jnp.broadcast_to(x[:, i : i + 1], x.shape)


def tree_sum(terms):
    terms = list(terms)
    while len(terms) > 1:
        terms = [terms[i] + terms[i + 1] if i + 1 < len(terms) else terms[i] for i in range(0, len(terms), 2)]
    return terms[0]


def invert8(columns):
    sub = lax.broadcasted_iota(jnp.int32, (8, 128), 0)
    columns = list(columns)
    for p in range(0, 8, 2):
        x, y = columns[p], columns[p + 1]
        a, b, c = row_of(x, p), row_of(y, p), row_of(y, p + 1)
        scale = 1.0 / (a * c - b * b)
        first, second = sub == p, sub == p + 1
        pivot_rows = jnp.logical_or(first, second)
        hu = jnp.where(first, c, jnp.where(second, -b, y * b - x * c))
        hv = jnp.where(first, -b, jnp.where(second, a, x * b - y * a))
        for j in range(8):
            if j in (p, p + 1):
                continue
            u, v = row_of(columns[j], p), row_of(columns[j], p + 1)
            columns[j] = jnp.where(pivot_rows, 0.0, columns[j]) + (hu * u + hv * v) * scale
        columns[p] = hu * scale
        columns[p + 1] = hv * scale
    return columns


def gauss_jordan(tiles, offset):
    count, parts = len(tiles), len(tiles[0])
    sub = lax.broadcasted_iota(jnp.int32, (8, 128), 0)
    lane = lax.broadcasted_iota(jnp.int32, (8, 128), 1)
    for k in range(count):
        start = offset + 8 * k
        block = jnp.logical_and(lane >= start, lane < start + 8)
        inverse = invert8([col_of(tiles[k][0], start + j) for j in range(8)])
        pivot = []
        for l in range(parts):
            value = tiles[k][l]
            if l == 0:
                value = jnp.where(block, jnp.where(lane - start == sub, 1.0, 0.0), value)
            pivot.append(tree_sum([inverse[j] * row_of(value, j) for j in range(8)]))
        rows = [[row_of(pivot[l], j) for j in range(8)] for l in range(parts)]
        for i in [i % count for i in range(k + 1, k + count)]:
            factors = [col_of(tiles[i][0], start + j) for j in range(8)]
            fresh = []
            for l in range(parts):
                base = tiles[i][l]
                if l == 0:
                    base = jnp.where(block, 0.0, base)
                fresh.append(base - tree_sum([factors[j] * rows[l][j] for j in range(8)]))
            tiles[i] = fresh
        tiles[k] = pivot
    return tiles


def packed(m):
    return [
        m[0:B, 0:128],
        jnp.concatenate([m[0:B, 128:H], m[128:H, 128:H]], axis=1),
        jnp.concatenate([m[B:128, 128:H], m[B:128, B:128]], axis=1),
    ]


def tree_kernel(
    sizes, state_in, source_in, rate_in, jac_in, lift_in, sep, leaf_in, out_ref,
    state, source, rate, jac, lift, leaf, in_sem,
    psb, eb, oob, one, two, three, tt, gg, xh, xl, xv, xout, edge_rows, halo_rows, edge_cols, halo_cols,
    up_send, up_recv, halo_send, halo_recv, down_send, down_recv,
):
    n_axial, n_azim, n_bank = sizes
    total = n_axial * n_azim * n_bank
    merges = total.bit_length() - 1
    local = merges - 1
    i_axial, i_azim, i_bank = lax.axis_index("axial"), lax.axis_index("azim"), lax.axis_index("bank")
    me = (i_axial * n_azim + i_azim) * n_bank + i_bank
    channels, rows_here, cells = state.shape

    def device(n):
        return (n // (n_azim * n_bank), (n // n_bank) % n_azim, n % n_bank)

    def field(level):
        bit = level if level < local else merges - 1
        azim_top = (n_bank * n_azim).bit_length() - 2
        if n_azim == 8 and bit == azim_top:
            return bit - 2, 3
        if n_axial == 32 and bit == azim_top + 3:
            return bit - 2, 3
        if n_axial == 32 and bit == azim_top + 5:
            return bit - 1, 2
        return bit, 1

    exchanges = [l for l in range(merges + 1) if l != local]

    def partner_at(level):
        low, width = field(level)
        value = (me // (1 << low)) % (1 << width)
        return me + ((1 << width) - 1 - 2 * value) * (1 << low)

    def partner(level):
        n = partner_at(0)
        for l in exchanges[1:]:
            n = jnp.where(level == l, partner_at(l), n)
        return n

    def first_slot(level):
        slot = jnp.int32(0)
        for l in range(merges + 1):
            bit = (me // (1 << l)) % 2
            here = 1 if l == local else (0 if l == merges else (1 - bit if l == merges - 2 else bit))
            slot = jnp.where(level == l, here, slot)
        return slot

    def piece(which, level, slot):
        if which == 0:
            return psb.at[level, slot, :, 0:256]
        if which == 1:
            return psb.at[level, slot, :, 256:384]
        return (eb if which == 2 else oob).at[level, slot]

    def upward(level, which, to):
        return pltpu.make_async_remote_copy(
            src_ref=piece(which, level, 0),
            dst_ref=piece(which, level, 1),
            send_sem=up_send.at[level, which],
            recv_sem=up_recv.at[level, which],
            device_id=to,
            device_id_type=MESH,
        )

    def downward():
        return pltpu.make_async_remote_copy(
            src_ref=xout.at[0],
            dst_ref=xout.at[1],
            send_sem=down_send,
            recv_sem=down_recv,
            device_id=device(partner_at(0)),
            device_id_type=MESH,
        )

    left = (i_axial, lax.rem(i_azim + n_azim - 1, n_azim), i_bank)
    right = (i_axial, lax.rem(i_azim + 1, n_azim), i_bank)
    above = (i_axial - 1, i_azim, i_bank)
    below = (i_axial + 1, i_azim, i_bank)
    has_above, has_below = i_axial > 0, i_axial < n_axial - 1

    def halo(which):
        src, dst, to = (
            (edge_rows.at[0], halo_rows.at[1], above),
            (edge_rows.at[1], halo_rows.at[0], below),
            (edge_cols.at[0], halo_cols.at[1], left),
            (edge_cols.at[1], halo_cols.at[0], right),
        )[which]
        return pltpu.make_async_remote_copy(
            src_ref=src,
            dst_ref=dst,
            send_sem=halo_send.at[which],
            recv_sem=halo_recv.at[which],
            device_id=to,
            device_id_type=MESH,
        )

    loads = [
        pltpu.make_async_copy(src, dst, in_sem.at[i])
        for i, (src, dst) in enumerate(
            ((leaf_in, leaf), (state_in, state), (source_in, source), (lift_in, lift), (rate_in, rate), (jac_in, jac))
        )
    ]
    for load in loads:
        load.start()
    halo_rows[...] = jnp.zeros_like(halo_rows)
    barrier = pltpu.get_barrier_semaphore()

    def greet(to):
        pl.semaphore_signal(barrier, inc=1, device_id=to, device_id_type=MESH)

    greet(left)
    greet(right)
    greet(device(partner_at(0)))
    pl.when(has_above)(lambda: greet(above))
    pl.when(has_below)(lambda: greet(below))

    @pl.when(i_bank == 0)
    def _():
        for level in exchanges[1:]:
            greet(device(partner_at(level)))

    loads[1].wait()
    lane128 = lax.broadcasted_iota(jnp.int32, (channels, 128), 1)
    edge_rows[0] = state[:, 0, :]
    edge_rows[1] = state[:, rows_here - 1, :]
    first_cols = jnp.zeros((channels, 128), F32)
    last_cols = jnp.zeros((channels, 128), F32)
    for r in range(rows_here):
        head, tail = state[:, r, 0:128], state[:, r, cells - 128 : cells]
        first_cols = jnp.where(lane128 == r, pltpu.roll(head, r, 1) if r else head, first_cols)
        last_cols = jnp.where(lane128 == r, pltpu.roll(tail, r + 1, 1), last_cols)
    edge_cols[0] = first_cols
    edge_cols[1] = last_cols

    def put(ref, level, parts):
        for l in range(3):
            ref[level, 0, :, 128 * l : 128 * l + 128] = parts[l]

    loads[0].wait()
    put(psb, 0, packed(leaf[H:, H:]))
    put(oob, 0, packed(leaf[:H, :H]))
    eb[0, 0, :, 0:H] = leaf[H:, :H]
    eb[0, 0, :, H:W] = jnp.zeros((H, W - H), F32)
    psb[local, 1] = jnp.zeros((B, 2 * H), F32)
    oob[local, 1] = jnp.zeros((B, 2 * H), F32)
    eb[local, 1] = jnp.zeros((H, W), F32)
    three[...] = jnp.zeros((B, 2 * B), F32)

    friends = 3 + jnp.where(has_above, 1, 0) + jnp.where(has_below, 1, 0)
    friends = friends + jnp.where(i_bank == 0, len(exchanges) - 1, 0)
    pl.semaphore_wait(barrier, friends)

    @pl.when(i_bank == 1)
    def _():
        for which in (0, 1, 3):
            upward(0, which, device(partner_at(0))).start()

    pl.when(has_above)(lambda: halo(0).start())
    pl.when(has_below)(lambda: halo(1).start())
    halo(2).start()
    halo(3).start()

    def front():
        pl.when(has_below)(lambda: halo(0).wait_recv())
        pl.when(has_above)(lambda: halo(1).wait_recv())
        halo(2).wait_recv()
        halo(3).wait_recv()
        for load in loads[2:]:
            load.wait()
        lane = lax.broadcasted_iota(jnp.int32, (channels, cells), 1)
        lane6 = lax.broadcasted_iota(jnp.int32, (sep.shape[0], cells), 1)
        jacobian = jac[...]
        rhs = jnp.zeros((channels, sep.shape[0]), F32)
        for r in range(rows_here):
            here = state[:, r, :]
            up = state[:, r - 1, :] if r else halo_rows[0]
            down = state[:, r + 1, :] if r < rows_here - 1 else halo_rows[1]
            before = jnp.where(lane == 0, halo_cols[0][:, r : r + 1], pltpu.roll(here, 1, 1))
            after = jnp.where(lane == cells - 1, halo_cols[1][:, r : r + 1], pltpu.roll(here, cells - 1, 1))
            reaction = mtn(jacobian, rate[r : r + 1, :] * here)
            residual = source[:, r, :] - reaction - diffusion * (4.0 * here - (up + down + before + after))
            picks = jnp.where(lane6 + r * cells == sep[...], 1.0, 0.0)
            rhs = rhs + mnt(residual, picks + lift[:, r, :])
        for c in range(3):
            eb[0, 0, c * channels : (c + 1) * channels, H : H + 1] = rhs[:, c + 3 : c + 4]
            eb[0, 0, c * channels : (c + 1) * channels, H + 1 : H + 2] = rhs[:, c : c + 1]

    @pl.when(i_bank == 1)
    def _():
        front()
        upward(0, 2, device(partner_at(0))).start()

    def ascend(level, carry):
        first = first_slot(level)
        second = 1 - first
        above = device(partner(level + 1))

        @pl.when(level != local)
        def _():
            upward(level, 0, left).wait_recv()

        def both(i, l):
            rows, lanes = pl.ds(8 * i, 8), pl.ds(128 * l, 128)
            return psb[level, 0, rows, lanes] + psb[level, 1, rows, lanes]

        tiles = gauss_jordan([[both(i, 0), both(i, 1)] for i in range(8)], 0)
        for i in range(8):
            for l in range(2):
                one[8 * i : 8 * i + 8, 128 * l : 128 * l + 128] = tiles[i][l]

        @pl.when(level != local)
        def _():
            upward(level, 1, left).wait_recv()

        lane = lax.broadcasted_iota(jnp.int32, (B, 128), 1)
        head = psb[level, 0, :, 0:256] + psb[level, 1, :, 0:256]
        k12, k13, k33 = head[:, B:128], head[:, 128:H], head[:, H:]
        update = mtn(k12, one[...])
        two[...] = (
            psb[level, 0, :, 256:384] + psb[level, 1, :, 256:384] - jnp.where(lane < B, update[:, 128:], update[:, :128])
        )
        s23 = two[:, 0:B]
        tiles = gauss_jordan([[two[8 * i : 8 * i + 8, :]] for i in range(8)], B)
        corner = k33 - mtn(k13, one[:, 128:H])
        for i in range(8):
            two[8 * i : 8 * i + 8, :] = tiles[i][0]
        three[:, 0:B] = corner - mtn(s23, two[:, 0:B])

        pl.when(level == 0)(front)

        @pl.when(level != local)
        def _():
            upward(level, 2, left).wait_recv()

        lane = lax.broadcasted_iota(jnp.int32, (H, 128), 1)
        e_first, e_second = eb[level, first], eb[level, second]
        tail_first, tail_second = e_first[:, 128:W], e_second[:, 128:W]
        outer_f = [tail_first, tail_second]
        tail_first = jnp.where(lane == B, tail_first + tail_second, jnp.where(lane < B, tail_first, 0.0))
        e = jnp.concatenate([e_second, e_first[:, 0:128], tail_first], axis=1)
        m1 = mtn(one[:, 0:H], e[0:B])
        t2 = e[B:128] - m1[B:128]
        m2 = mtn(two[...], t2)
        tt[0:B] = e[0:B]
        tt[B:128] = t2
        tt[128:H] = e[128:H] - m1[128:H] - m2[0:B]
        gg[0:B] = m1[0:B]
        gg[B:128] = m2[B:128]
        low = gauss_jordan([[three[8 * i : 8 * i + 8, :]] for i in range(8)], 0)
        for i in range(8):
            three[8 * i : 8 * i + 8, :] = low[i][0]

        @pl.when(jnp.logical_and(level != local, level != merges))
        def _():
            upward(level, 3, left).wait_recv()

        gg[128:H] = mm(three[:, 0:B], tt[128:H])
        parts = packed(mtn(tt[:, 0:H], gg[:, 0:H]))
        for l in range(3):
            lanes = pl.ds(128 * l, 128)
            psb[level + 1, 0, :, lanes] = oob[level, second, :, lanes] - parts[l]

        send = jnp.logical_and(level < merges, level + 1 != local)

        @pl.when(send)
        def _():
            upward(level + 1, 0, above).start()
            upward(level + 1, 1, above).start()

        cross = mtn(tt[:, 0:H], gg[:, W:])
        eb[level + 1, 0, :, 0:128] = -cross[:, 0:128]
        outer = mtn(tt[:, W : W + H], gg[:, W:])
        shared_f = pltpu.roll(outer_f[1], 127, 1) - cross[:, 128:W]
        outer_f = outer_f[0] - pltpu.roll(outer[:, 128:W], 1, 1)
        eb[level + 1, 0, :, 128:W] = jnp.where(
            lane < B, -cross[:, 128:W], jnp.where(lane == B, shared_f, jnp.where(lane == B + 1, outer_f, 0.0))
        )

        @pl.when(send)
        def _():
            upward(level + 1, 2, above).start()

        parts = packed(outer)
        for l in range(3):
            lanes = pl.ds(128 * l, 128)
            oob[level + 1, 0, :, lanes] = oob[level, first, :, lanes] - parts[l]

        @pl.when(jnp.logical_and(send, level + 1 != merges))
        def _():
            upward(level + 1, 3, above).start()

        x3 = gg[128:H]
        x2 = gg[B:128] - mm(two[:, 0:B], x3)
        x1 = gg[0:B] - mm(one[:, B:128], x2) - mm(one[:, 128:H], x3)
        for r, x in enumerate((x1, x2, x3)):
            high, low = halves(x)
            xh[level, B * r : B * r + B] = high
            xl[level, B * r : B * r + B] = low
        return carry

    lane8 = lax.broadcasted_iota(jnp.int32, (8, W), 1)

    def descend(i, carry):
        level = merges - i
        first = first_slot(level)
        x = [jnp.where(lane8 < H, -xv[level + 1, q], jnp.where(lane8 == H, 1.0 - q, 0.0)) for q in (1, 0)]
        high, low = halves(jnp.concatenate(x, axis=1))
        y = mnt_narrow(high, xh[level]) + (mnt_narrow(low, xh[level]) + mnt_narrow(high, xl[level]))
        xv[level, 0] = xv[level + 1, first]
        xv[level, 1, :, 0:H] = y
        return carry

    def wait_up(level, carry):
        @pl.when(level != local)
        def _():
            for which in range(3):
                upward(level, which, left).wait_send()

        @pl.when(jnp.logical_and(level != local, level != merges))
        def _():
            upward(level, 3, left).wait_send()

        return carry

    @pl.when(i_bank == 0)
    def _():
        lax.fori_loop(0, merges + 1, ascend, 0)
        xv[...] = jnp.zeros_like(xv)
        lax.fori_loop(0, merges + 1, descend, 0)
        xout[0, 0] = xv[1, 1 - first_slot(0)]
        xout[0, 1] = xv[0, 1]
        downward().start()
        out_ref[:, 0:H] = xv[0, 0, 0:1, 0:H]
        out_ref[:, H:] = xv[0, 1, 0:1, 0:H]
        lax.fori_loop(1, merges + 1, wait_up, 0)
        downward().wait_send()

    @pl.when(i_bank == 1)
    def _():
        for which in range(4):
            upward(0, which, left).wait_send()
        downward().wait_recv()
        out_ref[:, 0:H] = xout[1, 0, 0:1, 0:H]
        out_ref[:, H:] = xout[1, 1, 0:1, 0:H]

    pl.when(has_above)(lambda: halo(0).wait_send())
    pl.when(has_below)(lambda: halo(1).wait_send())
    halo(2).wait_send()
    halo(3).wait_send()


def solve_tree(sizes, state, source, rate, jac, lift, sep, leaf):
    total = sizes[0] * sizes[1] * sizes[2]
    slots = total.bit_length() + 1
    channels, rows, cells = state.shape
    vmem, hbm = pl.BlockSpec(memory_space=pltpu.VMEM), pl.BlockSpec(memory_space=pltpu.HBM)
    return pl.pallas_call(
        functools.partial(tree_kernel, sizes),
        out_shape=jax.ShapeDtypeStruct((1, 2 * H), F32),
        in_specs=[hbm] * 5 + [vmem, hbm],
        out_specs=vmem,
        scratch_shapes=[
            *(pltpu.VMEM(x.shape, F32) for x in (state, source, rate, jac, lift, leaf)),
            pltpu.SemaphoreType.DMA((6,)),
            pltpu.VMEM((slots, 2, B, 2 * H), F32),
            pltpu.VMEM((slots, 2, H, W), F32),
            pltpu.VMEM((slots, 2, B, 2 * H), F32),
            pltpu.VMEM((B, 256), F32),
            pltpu.VMEM((B, 128), F32),
            pltpu.VMEM((B, 128), F32),
            pltpu.VMEM((H, 2 * W), F32),
            pltpu.VMEM((H, 2 * W), F32),
            pltpu.VMEM((slots, H, 2 * W), BF16),
            pltpu.VMEM((slots, H, 2 * W), BF16),
            pltpu.VMEM((slots, 2, 8, W), F32),
            pltpu.VMEM((2, 2, 8, W), F32),
            pltpu.VMEM((2, channels, cells), F32),
            pltpu.VMEM((2, channels, cells), F32),
            pltpu.VMEM((2, channels, 128), F32),
            pltpu.VMEM((2, channels, 128), F32),
            pltpu.SemaphoreType.DMA((slots, 4)),
            pltpu.SemaphoreType.DMA((slots, 4)),
            pltpu.SemaphoreType.DMA((4,)),
            pltpu.SemaphoreType.DMA((4,)),
            pltpu.SemaphoreType.DMA,
            pltpu.SemaphoreType.DMA,
        ],
        compiler_params=pltpu.CompilerParams(
            collective_id=0, has_side_effects=True, vmem_limit_bytes=48 * 1024 * 1024
        ),
    )(*(pltpu.with_memory_space_constraint(x, pltpu.HBM) for x in (state, source, rate, jac, lift)), sep, pltpu.with_memory_space_constraint(leaf, pltpu.HBM))


def body(sizes, adjoint_state, adjoint_source, reaction_rate, jacobian, lifting, separator, leaf_schur):
    answer = solve_tree(
        sizes,
        adjoint_state[0],
        adjoint_source[0],
        reaction_rate[0],
        jacobian[0],
        lifting[0],
        separator.reshape(-1, 1),
        leaf_schur.reshape(2 * H, 2 * H),
    )
    return answer.reshape(1, 1, 1, 2 * H)


def solution(mesh):
    sizes = (mesh.shape["axial"], mesh.shape["azim"], mesh.shape["bank"])
    in_specs = (
        P("bank", None, "axial", "azim"),
        P("bank", None, "axial", "azim"),
        P("bank", "axial", "azim"),
        P("bank", None, None),
        P("bank", None, "axial", "azim"),
        P("axial", "azim", "bank", None),
        P("axial", "azim", "bank", None, None),
    )
    out_specs = P("axial", "azim", "bank", None)
    return jax.shard_map(
        functools.partial(body, sizes), mesh=mesh, in_specs=in_specs, out_specs=out_specs, check_vma=False
    )
```

```python
import functools

import jax
import jax.numpy as jnp
from jax import lax
from jax.experimental import pallas as pl
from jax.experimental.pallas import tpu as pltpu
from jax.sharding import PartitionSpec as P

highest = lax.Precision.HIGH
diffusion = 0.5
F32 = jnp.float32
BF16 = jnp.bfloat16
MESH = pl.DeviceIdType.MESH
H = 192
B = 64
W = 256


def mm(a, b):
    return lax.dot_general(a, b, (((1,), (0,)), ((), ())), precision=highest, preferred_element_type=F32)


def mtn(a, b):
    return lax.dot_general(a, b, (((0,), (0,)), ((), ())), precision=highest, preferred_element_type=F32)


def mnt(a, b):
    return lax.dot_general(a, b, (((1,), (1,)), ((), ())), precision=highest, preferred_element_type=F32)


def mnt_narrow(a, b):
    return lax.dot_general(a, b, (((1,), (1,)), ((), ())), preferred_element_type=F32)


def halves(x):
    high = x.astype(BF16)
    return high, (x - high.astype(F32)).astype(BF16)


def row_of(x, i):
    return jnp.broadcast_to(x[i : i + 1, :], x.shape)


def col_of(x, i):
    return jnp.take_along_axis(x, jnp.full(x.shape, i, jnp.int32), axis=1, mode="promise_in_bounds")


def tree_sum(terms):
    terms = list(terms)
    while len(terms) > 1:
        terms = [terms[i] + terms[i + 1] if i + 1 < len(terms) else terms[i] for i in range(0, len(terms), 2)]
    return terms[0]


def invert8(columns):
    sub = lax.broadcasted_iota(jnp.int32, (8, 128), 0)
    columns = list(columns)
    for p in range(0, 8, 2):
        x, y = columns[p], columns[p + 1]
        a, b, c = row_of(x, p), row_of(y, p), row_of(y, p + 1)
        scale = 1.0 / (a * c - b * b)
        first, second = sub == p, sub == p + 1
        pivot_rows = jnp.logical_or(first, second)
        hu = jnp.where(first, c, jnp.where(second, -b, y * b - x * c))
        hv = jnp.where(first, -b, jnp.where(second, a, x * b - y * a))
        for j in range(8):
            if j in (p, p + 1):
                continue
            u, v = row_of(columns[j], p), row_of(columns[j], p + 1)
            columns[j] = jnp.where(pivot_rows, 0.0, columns[j]) + (hu * u + hv * v) * scale
        columns[p] = hu * scale
        columns[p + 1] = hv * scale
    return columns


def gauss_jordan(tiles, offset):
    count, parts = len(tiles), len(tiles[0])
    sub = lax.broadcasted_iota(jnp.int32, (8, 128), 0)
    lane = lax.broadcasted_iota(jnp.int32, (8, 128), 1)

    def times(columns, rows):
        return tree_sum([c * r for c, r in zip(columns, rows)])

    def spread(value):
        return [row_of(value, j) for j in range(8)]

    def columns_of(value, start):
        return [col_of(value, start + j) for j in range(8)]

    for p in range(0, count, 2):
        q = p + 1
        start = offset + 8 * p
        block = jnp.logical_and(lane >= start, lane < start + 16)
        c11, c12 = columns_of(tiles[p][0], start), columns_of(tiles[p][0], start + 8)
        c21, c22 = columns_of(tiles[q][0], start), columns_of(tiles[q][0], start + 8)
        i1 = invert8(c11)
        y = [times(i1, spread(c12[j])) for j in range(8)]
        corner = [c22[j] - times(c21, spread(y[j])) for j in range(8)]
        upper, lower = list(tiles[p]), list(tiles[q])
        upper[0] = jnp.where(block, jnp.where(lane - start == sub, 1.0, 0.0), upper[0])
        lower[0] = jnp.where(block, jnp.where(lane - start - 8 == sub, 1.0, 0.0), lower[0])
        upper = [times(i1, spread(t)) for t in upper]
        lower = [t - times(c21, spread(u)) for t, u in zip(lower, upper)]
        i2 = invert8(corner)
        lower = [times(i2, spread(t)) for t in lower]
        lower_rows = [spread(t) for t in lower]
        upper = [u - times(y, rows) for u, rows in zip(upper, lower_rows)]
        upper_rows = [spread(t) for t in upper]
        for i in [i % count for i in range(q + 1, p + count)]:
            factors = columns_of(tiles[i][0], start) + columns_of(tiles[i][0], start + 8)
            fresh = []
            for l in range(parts):
                base = tiles[i][l]
                if l == 0:
                    base = jnp.where(block, 0.0, base)
                fresh.append(base - times(factors, upper_rows[l] + lower_rows[l]))
            tiles[i] = fresh
        tiles[p], tiles[q] = upper, lower
    return tiles


def packed(m):
    return [
        m[0:B, 0:128],
        jnp.concatenate([m[0:B, 128:H], m[128:H, 128:H]], axis=1),
        jnp.concatenate([m[B:128, 128:H], m[B:128, B:128]], axis=1),
    ]


def tree_kernel(
    sizes, state_in, source_in, rate_in, jac_in, lift_in, sep, leaf_in, out_ref,
    state, source, rate, jac, lift, leaf, in_sem,
    psb, eb, oob, one, two, three, tt, gg, xh, xl, xv, xout, edge_rows, halo_rows, edge_cols, halo_cols,
    up_send, up_recv, halo_send, halo_recv, down_send, down_recv,
):
    n_axial, n_azim, n_bank = sizes
    total = n_axial * n_azim * n_bank
    merges = total.bit_length() - 1
    local = merges - 1
    i_axial, i_azim, i_bank = lax.axis_index("axial"), lax.axis_index("azim"), lax.axis_index("bank")
    me = (i_axial * n_azim + i_azim) * n_bank + i_bank
    channels, rows_here, cells = state.shape

    def device(n):
        return (n // (n_azim * n_bank), (n // n_bank) % n_azim, n % n_bank)

    def field(level):
        bit = level if level < local else merges - 1
        azim_top = (n_bank * n_azim).bit_length() - 2
        if n_azim == 8 and bit == azim_top:
            return bit - 2, 3
        if n_axial == 32 and bit == azim_top + 3:
            return bit - 2, 3
        if n_axial == 32 and bit == azim_top + 5:
            return bit - 1, 2
        return bit, 1

    exchanges = [l for l in range(merges + 1) if l != local]

    def partner_at(level):
        low, width = field(level)
        value = (me // (1 << low)) % (1 << width)
        return me + ((1 << width) - 1 - 2 * value) * (1 << low)

    def partner(level):
        n = partner_at(0)
        for l in exchanges[1:]:
            n = jnp.where(level == l, partner_at(l), n)
        return n

    def first_slot(level):
        slot = jnp.int32(0)
        for l in range(merges + 1):
            bit = (me // (1 << l)) % 2
            here = 1 if l == local else (0 if l == merges else (1 - bit if l == merges - 2 else bit))
            slot = jnp.where(level == l, here, slot)
        return slot

    def piece(which, level, slot):
        if which == 0:
            return psb.at[level, slot, :, 0:256]
        if which == 1:
            return psb.at[level, slot, :, 256:384]
        return (eb if which == 2 else oob).at[level, slot]

    def upward(level, which, to):
        return pltpu.make_async_remote_copy(
            src_ref=piece(which, level, 0),
            dst_ref=piece(which, level, 1),
            send_sem=up_send.at[level, which],
            recv_sem=up_recv.at[level, which],
            device_id=to,
            device_id_type=MESH,
        )

    def downward():
        return pltpu.make_async_remote_copy(
            src_ref=xout.at[0],
            dst_ref=xout.at[1],
            send_sem=down_send,
            recv_sem=down_recv,
            device_id=device(partner_at(0)),
            device_id_type=MESH,
        )

    left = (i_axial, lax.rem(i_azim + n_azim - 1, n_azim), i_bank)
    right = (i_axial, lax.rem(i_azim + 1, n_azim), i_bank)
    above = (i_axial - 1, i_azim, i_bank)
    below = (i_axial + 1, i_azim, i_bank)
    has_above, has_below = i_axial > 0, i_axial < n_axial - 1

    def halo(which):
        src, dst, to = (
            (edge_rows.at[0], halo_rows.at[1], above),
            (edge_rows.at[1], halo_rows.at[0], below),
            (edge_cols.at[0], halo_cols.at[1], left),
            (edge_cols.at[1], halo_cols.at[0], right),
        )[which]
        return pltpu.make_async_remote_copy(
            src_ref=src,
            dst_ref=dst,
            send_sem=halo_send.at[which],
            recv_sem=halo_recv.at[which],
            device_id=to,
            device_id_type=MESH,
        )

    loads = [
        pltpu.make_async_copy(src, dst, in_sem.at[i])
        for i, (src, dst) in enumerate(
            ((leaf_in, leaf), (state_in, state), (source_in, source), (lift_in, lift), (rate_in, rate), (jac_in, jac))
        )
    ]
    for load in loads:
        load.start()
    halo_rows[...] = jnp.zeros_like(halo_rows)
    barrier = pltpu.get_barrier_semaphore()

    def greet(to):
        pl.semaphore_signal(barrier, inc=1, device_id=to, device_id_type=MESH)

    greet(left)
    greet(right)
    greet(device(partner_at(0)))
    pl.when(has_above)(lambda: greet(above))
    pl.when(has_below)(lambda: greet(below))

    @pl.when(i_bank == 0)
    def _():
        for level in exchanges[1:]:
            greet(device(partner_at(level)))

    loads[1].wait()
    lane128 = lax.broadcasted_iota(jnp.int32, (channels, 128), 1)
    edge_rows[0] = state[:, 0, :]
    edge_rows[1] = state[:, rows_here - 1, :]
    first_cols = jnp.zeros((channels, 128), F32)
    last_cols = jnp.zeros((channels, 128), F32)
    for r in range(rows_here):
        head, tail = state[:, r, 0:128], state[:, r, cells - 128 : cells]
        first_cols = jnp.where(lane128 == r, pltpu.roll(head, r, 1) if r else head, first_cols)
        last_cols = jnp.where(lane128 == r, pltpu.roll(tail, r + 1, 1), last_cols)
    edge_cols[0] = first_cols
    edge_cols[1] = last_cols

    def put(ref, level, parts):
        for l in range(3):
            ref[level, 0, :, 128 * l : 128 * l + 128] = parts[l]

    loads[0].wait()
    put(psb, 0, packed(leaf[H:, H:]))
    put(oob, 0, packed(leaf[:H, :H]))
    eb[0, 0, :, 0:H] = leaf[H:, :H]
    eb[0, 0, :, H:W] = jnp.zeros((H, W - H), F32)
    psb[local, 1] = jnp.zeros((B, 2 * H), F32)
    oob[local, 1] = jnp.zeros((B, 2 * H), F32)
    eb[local, 1] = jnp.zeros((H, W), F32)
    three[...] = jnp.zeros((B, 2 * B), F32)

    friends = 3 + jnp.where(has_above, 1, 0) + jnp.where(has_below, 1, 0)
    friends = friends + jnp.where(i_bank == 0, len(exchanges) - 1, 0)
    pl.semaphore_wait(barrier, friends)

    @pl.when(i_bank == 1)
    def _():
        for which in (0, 1, 3):
            upward(0, which, device(partner_at(0))).start()

    pl.when(has_above)(lambda: halo(0).start())
    pl.when(has_below)(lambda: halo(1).start())
    halo(2).start()
    halo(3).start()

    def front():
        pl.when(has_below)(lambda: halo(0).wait_recv())
        pl.when(has_above)(lambda: halo(1).wait_recv())
        halo(2).wait_recv()
        halo(3).wait_recv()
        for load in loads[2:]:
            load.wait()
        lane = lax.broadcasted_iota(jnp.int32, (channels, cells), 1)
        lane6 = lax.broadcasted_iota(jnp.int32, (sep.shape[0], cells), 1)
        jacobian = jac[...]
        rhs = jnp.zeros((channels, sep.shape[0]), F32)
        for r in range(rows_here):
            here = state[:, r, :]
            up = state[:, r - 1, :] if r else halo_rows[0]
            down = state[:, r + 1, :] if r < rows_here - 1 else halo_rows[1]
            before = jnp.where(lane == 0, halo_cols[0][:, r : r + 1], pltpu.roll(here, 1, 1))
            after = jnp.where(lane == cells - 1, halo_cols[1][:, r : r + 1], pltpu.roll(here, cells - 1, 1))
            reaction = mtn(jacobian, rate[r : r + 1, :] * here)
            residual = source[:, r, :] - reaction - diffusion * (4.0 * here - (up + down + before + after))
            picks = jnp.where(lane6 + r * cells == sep[...], 1.0, 0.0)
            rhs = rhs + mnt(residual, picks + lift[:, r, :])
        for c in range(3):
            eb[0, 0, c * channels : (c + 1) * channels, H : H + 1] = rhs[:, c + 3 : c + 4]
            eb[0, 0, c * channels : (c + 1) * channels, H + 1 : H + 2] = rhs[:, c : c + 1]

    @pl.when(i_bank == 1)
    def _():
        front()
        upward(0, 2, device(partner_at(0))).start()

    def ascend(level, carry):
        first = first_slot(level)
        second = 1 - first
        above = device(partner(level + 1))

        @pl.when(level != local)
        def _():
            upward(level, 0, left).wait_recv()

        def both(i, l):
            rows, lanes = pl.ds(8 * i, 8), pl.ds(128 * l, 128)
            return psb[level, 0, rows, lanes] + psb[level, 1, rows, lanes]

        tiles = gauss_jordan([[both(i, 0), both(i, 1)] for i in range(8)], 0)
        for i in range(8):
            for l in range(2):
                one[8 * i : 8 * i + 8, 128 * l : 128 * l + 128] = tiles[i][l]

        @pl.when(level != local)
        def _():
            upward(level, 1, left).wait_recv()

        lane = lax.broadcasted_iota(jnp.int32, (B, 128), 1)
        head = psb[level, 0, :, 0:256] + psb[level, 1, :, 0:256]
        k12, k13, k33 = head[:, B:128], head[:, 128:H], head[:, H:]
        update = mtn(k12, one[...])
        two[...] = (
            psb[level, 0, :, 256:384] + psb[level, 1, :, 256:384] - jnp.where(lane < B, update[:, 128:], update[:, :128])
        )
        s23 = two[:, 0:B]
        tiles = gauss_jordan([[two[8 * i : 8 * i + 8, :]] for i in range(8)], B)
        corner = k33 - mtn(k13, one[:, 128:H])
        for i in range(8):
            two[8 * i : 8 * i + 8, :] = tiles[i][0]
        three[:, 0:B] = corner - mtn(s23, two[:, 0:B])

        pl.when(level == 0)(front)

        @pl.when(level != local)
        def _():
            upward(level, 2, left).wait_recv()

        lane = lax.broadcasted_iota(jnp.int32, (H, 128), 1)
        e_first, e_second = eb[level, first], eb[level, second]
        tail_first, tail_second = e_first[:, 128:W], e_second[:, 128:W]
        outer_f = [tail_first, tail_second]
        tail_first = jnp.where(lane == B, tail_first + tail_second, jnp.where(lane < B, tail_first, 0.0))
        e = jnp.concatenate([e_second, e_first[:, 0:128], tail_first], axis=1)
        m1 = mtn(one[:, 0:H], e[0:B])
        t2 = e[B:128] - m1[B:128]
        m2 = mtn(two[...], t2)
        tt[0:B] = e[0:B]
        tt[B:128] = t2
        tt[128:H] = e[128:H] - m1[128:H] - m2[0:B]
        gg[0:B] = m1[0:B]
        gg[B:128] = m2[B:128]
        low = gauss_jordan([[three[8 * i : 8 * i + 8, :]] for i in range(8)], 0)
        for i in range(8):
            three[8 * i : 8 * i + 8, :] = low[i][0]

        @pl.when(jnp.logical_and(level != local, level != merges))
        def _():
            upward(level, 3, left).wait_recv()

        gg[128:H] = mm(three[:, 0:B], tt[128:H])
        parts = packed(mtn(tt[:, 0:H], gg[:, 0:H]))
        for l in range(3):
            lanes = pl.ds(128 * l, 128)
            psb[level + 1, 0, :, lanes] = oob[level, second, :, lanes] - parts[l]

        send = jnp.logical_and(level < merges, level + 1 != local)

        @pl.when(send)
        def _():
            upward(level + 1, 0, above).start()
            upward(level + 1, 1, above).start()

        cross = mtn(tt[:, 0:H], gg[:, W:])
        eb[level + 1, 0, :, 0:128] = -cross[:, 0:128]
        outer = mtn(tt[:, W : W + H], gg[:, W:])
        shared_f = pltpu.roll(outer_f[1], 127, 1) - cross[:, 128:W]
        outer_f = outer_f[0] - pltpu.roll(outer[:, 128:W], 1, 1)
        eb[level + 1, 0, :, 128:W] = jnp.where(
            lane < B, -cross[:, 128:W], jnp.where(lane == B, shared_f, jnp.where(lane == B + 1, outer_f, 0.0))
        )

        @pl.when(send)
        def _():
            upward(level + 1, 2, above).start()

        parts = packed(outer)
        for l in range(3):
            lanes = pl.ds(128 * l, 128)
            oob[level + 1, 0, :, lanes] = oob[level, first, :, lanes] - parts[l]

        @pl.when(jnp.logical_and(send, level + 1 != merges))
        def _():
            upward(level + 1, 3, above).start()

        x3 = gg[128:H]
        x2 = gg[B:128] - mm(two[:, 0:B], x3)
        x1 = gg[0:B] - mm(one[:, B:128], x2) - mm(one[:, 128:H], x3)
        for r, x in enumerate((x1, x2, x3)):
            high, low = halves(x)
            xh[level, B * r : B * r + B] = high
            xl[level, B * r : B * r + B] = low
        return carry

    lane8 = lax.broadcasted_iota(jnp.int32, (8, W), 1)

    def descend(i, carry):
        level = merges - i
        first = first_slot(level)
        x = [jnp.where(lane8 < H, -xv[level + 1, q], jnp.where(lane8 == H, 1.0 - q, 0.0)) for q in (1, 0)]
        high, low = halves(jnp.concatenate(x, axis=1))
        y = mnt_narrow(high, xh[level]) + (mnt_narrow(low, xh[level]) + mnt_narrow(high, xl[level]))
        xv[level, 0] = xv[level + 1, first]
        xv[level, 1, :, 0:H] = y
        return carry

    def wait_up(level, carry):
        @pl.when(level != local)
        def _():
            for which in range(3):
                upward(level, which, left).wait_send()

        @pl.when(jnp.logical_and(level != local, level != merges))
        def _():
            upward(level, 3, left).wait_send()

        return carry

    @pl.when(i_bank == 0)
    def _():
        lax.fori_loop(0, merges + 1, ascend, 0)
        xv[...] = jnp.zeros_like(xv)
        lax.fori_loop(0, merges + 1, descend, 0)
        xout[0, 0] = xv[1, 1 - first_slot(0)]
        xout[0, 1] = xv[0, 1]
        downward().start()
        out_ref[:, 0:H] = xv[0, 0, 0:1, 0:H]
        out_ref[:, H:] = xv[0, 1, 0:1, 0:H]
        lax.fori_loop(1, merges + 1, wait_up, 0)
        downward().wait_send()

    @pl.when(i_bank == 1)
    def _():
        for which in range(4):
            upward(0, which, left).wait_send()
        downward().wait_recv()
        out_ref[:, 0:H] = xout[1, 0, 0:1, 0:H]
        out_ref[:, H:] = xout[1, 1, 0:1, 0:H]

    pl.when(has_above)(lambda: halo(0).wait_send())
    pl.when(has_below)(lambda: halo(1).wait_send())
    halo(2).wait_send()
    halo(3).wait_send()


def solve_tree(sizes, state, source, rate, jac, lift, sep, leaf):
    total = sizes[0] * sizes[1] * sizes[2]
    slots = total.bit_length() + 1
    channels, rows, cells = state.shape
    vmem, hbm = pl.BlockSpec(memory_space=pltpu.VMEM), pl.BlockSpec(memory_space=pltpu.HBM)
    return pl.pallas_call(
        functools.partial(tree_kernel, sizes),
        out_shape=jax.ShapeDtypeStruct((1, 2 * H), F32),
        in_specs=[hbm] * 5 + [vmem, hbm],
        out_specs=vmem,
        scratch_shapes=[
            *(pltpu.VMEM(x.shape, F32) for x in (state, source, rate, jac, lift, leaf)),
            pltpu.SemaphoreType.DMA((6,)),
            pltpu.VMEM((slots, 2, B, 2 * H), F32),
            pltpu.VMEM((slots, 2, H, W), F32),
            pltpu.VMEM((slots, 2, B, 2 * H), F32),
            pltpu.VMEM((B, 256), F32),
            pltpu.VMEM((B, 128), F32),
            pltpu.VMEM((B, 128), F32),
            pltpu.VMEM((H, 2 * W), F32),
            pltpu.VMEM((H, 2 * W), F32),
            pltpu.VMEM((slots, H, 2 * W), BF16),
            pltpu.VMEM((slots, H, 2 * W), BF16),
            pltpu.VMEM((slots, 2, 8, W), F32),
            pltpu.VMEM((2, 2, 8, W), F32),
            pltpu.VMEM((2, channels, cells), F32),
            pltpu.VMEM((2, channels, cells), F32),
            pltpu.VMEM((2, channels, 128), F32),
            pltpu.VMEM((2, channels, 128), F32),
            pltpu.SemaphoreType.DMA((slots, 4)),
            pltpu.SemaphoreType.DMA((slots, 4)),
            pltpu.SemaphoreType.DMA((4,)),
            pltpu.SemaphoreType.DMA((4,)),
            pltpu.SemaphoreType.DMA,
            pltpu.SemaphoreType.DMA,
        ],
        compiler_params=pltpu.CompilerParams(
            collective_id=0, has_side_effects=True, vmem_limit_bytes=48 * 1024 * 1024
        ),
    )(*(pltpu.with_memory_space_constraint(x, pltpu.HBM) for x in (state, source, rate, jac, lift)), sep, pltpu.with_memory_space_constraint(leaf, pltpu.HBM))


def body(sizes, adjoint_state, adjoint_source, reaction_rate, jacobian, lifting, separator, leaf_schur):
    answer = solve_tree(
        sizes,
        adjoint_state[0],
        adjoint_source[0],
        reaction_rate[0],
        jacobian[0],
        lifting[0],
        separator.reshape(-1, 1),
        leaf_schur.reshape(2 * H, 2 * H),
    )
    return answer.reshape(1, 1, 1, 2 * H)


def solution(mesh):
    sizes = (mesh.shape["axial"], mesh.shape["azim"], mesh.shape["bank"])
    in_specs = (
        P("bank", None, "axial", "azim"),
        P("bank", None, "axial", "azim"),
        P("bank", "axial", "azim"),
        P("bank", None, None),
        P("bank", None, "axial", "azim"),
        P("axial", "azim", "bank", None),
        P("axial", "azim", "bank", None, None),
    )
    out_specs = P("axial", "azim", "bank", None)
    return jax.shard_map(
        functools.partial(body, sizes), mesh=mesh, in_specs=in_specs, out_specs=out_specs, check_vma=False
    )
```

```python
import functools

import jax
import jax.numpy as jnp
from jax import lax
from jax.experimental import pallas as pl
from jax.experimental.pallas import tpu as pltpu
from jax.sharding import PartitionSpec as P

highest = lax.Precision.HIGH
diffusion = 0.5
F32 = jnp.float32
BF16 = jnp.bfloat16
MESH = pl.DeviceIdType.MESH
H = 192
B = 64
W = 256


def mm(a, b):
    return lax.dot_general(a, b, (((1,), (0,)), ((), ())), precision=highest, preferred_element_type=F32)


def mtn(a, b):
    return lax.dot_general(a, b, (((0,), (0,)), ((), ())), precision=highest, preferred_element_type=F32)


def mnt(a, b):
    return lax.dot_general(a, b, (((1,), (1,)), ((), ())), precision=highest, preferred_element_type=F32)


def mnt_narrow(a, b):
    return lax.dot_general(a, b, (((1,), (1,)), ((), ())), preferred_element_type=F32)


def halves(x):
    high = x.astype(BF16)
    return high, (x - high.astype(F32)).astype(BF16)


def row_of(x, i):
    return jnp.broadcast_to(x[i : i + 1, :], x.shape)


def col_of(x, i):
    return jnp.take_along_axis(x, jnp.full(x.shape, i, jnp.int32), axis=1, mode="promise_in_bounds")


def tree_sum(terms):
    terms = list(terms)
    while len(terms) > 1:
        terms = [terms[i] + terms[i + 1] if i + 1 < len(terms) else terms[i] for i in range(0, len(terms), 2)]
    return terms[0]


def invert8(columns):
    sub = lax.broadcasted_iota(jnp.int32, (8, 128), 0)
    columns = list(columns)
    for p in range(0, 8, 2):
        x, y = columns[p], columns[p + 1]
        a, b, c = row_of(x, p), row_of(y, p), row_of(y, p + 1)
        scale = 1.0 / (a * c - b * b)
        first, second = sub == p, sub == p + 1
        pivot_rows = jnp.logical_or(first, second)
        hu = jnp.where(first, c, jnp.where(second, -b, y * b - x * c))
        hv = jnp.where(first, -b, jnp.where(second, a, x * b - y * a))
        for j in range(8):
            if j in (p, p + 1):
                continue
            u, v = row_of(columns[j], p), row_of(columns[j], p + 1)
            columns[j] = jnp.where(pivot_rows, 0.0, columns[j]) + (hu * u + hv * v) * scale
        columns[p] = hu * scale
        columns[p + 1] = hv * scale
    return columns


def gauss_jordan(tiles, offset):
    count, parts = len(tiles), len(tiles[0])
    sub = lax.broadcasted_iota(jnp.int32, (8, 128), 0)
    lane = lax.broadcasted_iota(jnp.int32, (8, 128), 1)

    def times(columns, rows):
        return tree_sum([c * r for c, r in zip(columns, rows)])

    def spread(value):
        return [row_of(value, j) for j in range(8)]

    def columns_of(value, start):
        return [col_of(value, start + j) for j in range(8)]

    for p in range(0, count, 2):
        q = p + 1
        start = offset + 8 * p
        block = jnp.logical_and(lane >= start, lane < start + 16)
        c11, c12 = columns_of(tiles[p][0], start), columns_of(tiles[p][0], start + 8)
        c21, c22 = columns_of(tiles[q][0], start), columns_of(tiles[q][0], start + 8)
        i1 = invert8(c11)
        y = [times(i1, spread(c12[j])) for j in range(8)]
        corner = [c22[j] - times(c21, spread(y[j])) for j in range(8)]
        upper, lower = list(tiles[p]), list(tiles[q])
        upper[0] = jnp.where(block, jnp.where(lane - start == sub, 1.0, 0.0), upper[0])
        lower[0] = jnp.where(block, jnp.where(lane - start - 8 == sub, 1.0, 0.0), lower[0])
        upper = [times(i1, spread(t)) for t in upper]
        lower = [t - times(c21, spread(u)) for t, u in zip(lower, upper)]
        i2 = invert8(corner)
        lower = [times(i2, spread(t)) for t in lower]
        lower_rows = [spread(t) for t in lower]
        upper = [u - times(y, rows) for u, rows in zip(upper, lower_rows)]
        upper_rows = [spread(t) for t in upper]
        for i in [i % count for i in range(q + 1, p + count)]:
            factors = columns_of(tiles[i][0], start) + columns_of(tiles[i][0], start + 8)
            fresh = []
            for l in range(parts):
                base = tiles[i][l]
                if l == 0:
                    base = jnp.where(block, 0.0, base)
                fresh.append(base - times(factors, upper_rows[l] + lower_rows[l]))
            tiles[i] = fresh
        tiles[p], tiles[q] = upper, lower
    return tiles


def packed(m):
    return [
        m[0:B, 0:128],
        jnp.concatenate([m[0:B, 128:H], m[128:H, 128:H]], axis=1),
        jnp.concatenate([m[B:128, 128:H], m[B:128, B:128]], axis=1),
    ]


def tree_kernel(
    sizes, state_in, source_in, rate_in, jac_in, lift_in, sep, leaf_in, out_ref,
    state, source, rate, jac, lift, leaf, in_sem,
    psb, eb, oob, one, two, three, tt, gg, xh, xl, xv, xout, edge_rows, halo_rows, edge_cols, halo_cols,
    up_send, up_recv, halo_send, halo_recv, down_send, down_recv,
):
    n_axial, n_azim, n_bank = sizes
    total = n_axial * n_azim * n_bank
    merges = total.bit_length() - 1
    local = merges - 1
    i_axial, i_azim, i_bank = lax.axis_index("axial"), lax.axis_index("azim"), lax.axis_index("bank")
    me = (i_axial * n_azim + i_azim) * n_bank + i_bank
    channels, rows_here, cells = state.shape

    def device(n):
        return (n // (n_azim * n_bank), (n // n_bank) % n_azim, n % n_bank)

    def field(level):
        bit = level if level < local else merges - 1
        azim_top = (n_bank * n_azim).bit_length() - 2
        if n_azim == 8 and bit == azim_top:
            return bit - 2, 3
        if n_axial == 32 and bit == azim_top + 3:
            return bit - 2, 3
        if n_axial == 32 and bit == azim_top + 5:
            return bit - 1, 2
        return bit, 1

    exchanges = [l for l in range(merges + 1) if l != local]

    def partner_at(level):
        low, width = field(level)
        value = (me // (1 << low)) % (1 << width)
        return me + ((1 << width) - 1 - 2 * value) * (1 << low)

    def partner(level):
        n = partner_at(0)
        for l in exchanges[1:]:
            n = jnp.where(level == l, partner_at(l), n)
        return n

    def first_slot(level):
        slot = jnp.int32(0)
        for l in range(merges + 1):
            bit = (me // (1 << l)) % 2
            here = 1 if l == local else (0 if l == merges else (1 - bit if l == merges - 2 else bit))
            slot = jnp.where(level == l, here, slot)
        return slot

    def piece(which, level, slot):
        if which == 0:
            return psb.at[level, slot, :, 0:128]
        if which == 1:
            return psb.at[level, slot, :, 128:384]
        return (eb if which == 2 else oob).at[level, slot]

    def upward(level, which, to):
        return pltpu.make_async_remote_copy(
            src_ref=piece(which, level, 0),
            dst_ref=piece(which, level, 1),
            send_sem=up_send.at[level, which],
            recv_sem=up_recv.at[level, which],
            device_id=to,
            device_id_type=MESH,
        )

    def downward():
        return pltpu.make_async_remote_copy(
            src_ref=xout.at[0],
            dst_ref=xout.at[1],
            send_sem=down_send,
            recv_sem=down_recv,
            device_id=device(partner_at(0)),
            device_id_type=MESH,
        )

    left = (i_axial, lax.rem(i_azim + n_azim - 1, n_azim), i_bank)
    right = (i_axial, lax.rem(i_azim + 1, n_azim), i_bank)
    above = (i_axial - 1, i_azim, i_bank)
    below = (i_axial + 1, i_azim, i_bank)
    has_above, has_below = i_axial > 0, i_axial < n_axial - 1

    def halo(which):
        src, dst, to = (
            (edge_rows.at[0], halo_rows.at[1], above),
            (edge_rows.at[1], halo_rows.at[0], below),
            (edge_cols.at[0], halo_cols.at[1], left),
            (edge_cols.at[1], halo_cols.at[0], right),
        )[which]
        return pltpu.make_async_remote_copy(
            src_ref=src,
            dst_ref=dst,
            send_sem=halo_send.at[which],
            recv_sem=halo_recv.at[which],
            device_id=to,
            device_id_type=MESH,
        )

    loads = [
        pltpu.make_async_copy(src, dst, in_sem.at[i])
        for i, (src, dst) in enumerate(
            ((leaf_in, leaf), (state_in, state), (source_in, source), (lift_in, lift), (rate_in, rate), (jac_in, jac))
        )
    ]
    for load in loads:
        load.start()
    halo_rows[...] = jnp.zeros_like(halo_rows)
    barrier = pltpu.get_barrier_semaphore()

    def greet(to):
        pl.semaphore_signal(barrier, inc=1, device_id=to, device_id_type=MESH)

    greet(left)
    greet(right)
    greet(device(partner_at(0)))
    pl.when(has_above)(lambda: greet(above))
    pl.when(has_below)(lambda: greet(below))

    @pl.when(i_bank == 0)
    def _():
        for level in exchanges[1:]:
            greet(device(partner_at(level)))

    loads[1].wait()
    lane128 = lax.broadcasted_iota(jnp.int32, (channels, 128), 1)
    edge_rows[0] = state[:, 0, :]
    edge_rows[1] = state[:, rows_here - 1, :]
    first_cols = jnp.zeros((channels, 128), F32)
    last_cols = jnp.zeros((channels, 128), F32)
    for r in range(rows_here):
        head, tail = state[:, r, 0:128], state[:, r, cells - 128 : cells]
        first_cols = jnp.where(lane128 == r, pltpu.roll(head, r, 1) if r else head, first_cols)
        last_cols = jnp.where(lane128 == r, pltpu.roll(tail, r + 1, 1), last_cols)
    edge_cols[0] = first_cols
    edge_cols[1] = last_cols

    def put(ref, level, parts):
        for l in range(3):
            ref[level, 0, :, 128 * l : 128 * l + 128] = parts[l]

    loads[0].wait()
    put(psb, 0, packed(leaf[H:, H:]))
    put(oob, 0, packed(leaf[:H, :H]))
    eb[0, 0, :, 0:H] = leaf[H:, :H]
    eb[0, 0, :, H:W] = jnp.zeros((H, W - H), F32)
    psb[local, 1] = jnp.zeros((B, 2 * H), F32)
    oob[local, 1] = jnp.zeros((B, 2 * H), F32)
    eb[local, 1] = jnp.zeros((H, W), F32)
    three[...] = jnp.zeros((B, 2 * B), F32)

    friends = 3 + jnp.where(has_above, 1, 0) + jnp.where(has_below, 1, 0)
    friends = friends + jnp.where(i_bank == 0, len(exchanges) - 1, 0)
    pl.semaphore_wait(barrier, friends)

    @pl.when(i_bank == 1)
    def _():
        for which in (0, 1, 3):
            upward(0, which, device(partner_at(0))).start()

    pl.when(has_above)(lambda: halo(0).start())
    pl.when(has_below)(lambda: halo(1).start())
    halo(2).start()
    halo(3).start()

    def front():
        pl.when(has_below)(lambda: halo(0).wait_recv())
        pl.when(has_above)(lambda: halo(1).wait_recv())
        halo(2).wait_recv()
        halo(3).wait_recv()
        for load in loads[2:]:
            load.wait()
        lane = lax.broadcasted_iota(jnp.int32, (channels, cells), 1)
        lane6 = lax.broadcasted_iota(jnp.int32, (sep.shape[0], cells), 1)
        jacobian = jac[...]
        rhs = jnp.zeros((channels, sep.shape[0]), F32)
        for r in range(rows_here):
            here = state[:, r, :]
            up = state[:, r - 1, :] if r else halo_rows[0]
            down = state[:, r + 1, :] if r < rows_here - 1 else halo_rows[1]
            before = jnp.where(lane == 0, halo_cols[0][:, r : r + 1], pltpu.roll(here, 1, 1))
            after = jnp.where(lane == cells - 1, halo_cols[1][:, r : r + 1], pltpu.roll(here, cells - 1, 1))
            reaction = mtn(jacobian, rate[r : r + 1, :] * here)
            residual = source[:, r, :] - reaction - diffusion * (4.0 * here - (up + down + before + after))
            picks = jnp.where(lane6 + r * cells == sep[...], 1.0, 0.0)
            rhs = rhs + mnt(residual, picks + lift[:, r, :])
        for c in range(3):
            eb[0, 0, c * channels : (c + 1) * channels, H : H + 1] = rhs[:, c + 3 : c + 4]
            eb[0, 0, c * channels : (c + 1) * channels, H + 1 : H + 2] = rhs[:, c : c + 1]

    @pl.when(i_bank == 1)
    def _():
        front()
        upward(0, 2, device(partner_at(0))).start()

    def ascend(level, carry):
        first = first_slot(level)
        second = 1 - first
        above = device(partner(level + 1))

        @pl.when(level != local)
        def _():
            upward(level, 0, left).wait_recv()

        def both(i):
            rows = pl.ds(8 * i, 8)
            return psb[level, 0, rows, 0:128] + psb[level, 1, rows, 0:128]

        tiles = gauss_jordan([[both(i)] for i in range(8)], 0)
        for i in range(8):
            one[8 * i : 8 * i + 8, 0:128] = tiles[i][0]

        @pl.when(level != local)
        def _():
            upward(level, 1, left).wait_recv()

        lane = lax.broadcasted_iota(jnp.int32, (B, 128), 1)
        head = psb[level, 0, :, 0:256] + psb[level, 1, :, 0:256]
        k13, k33 = head[:, 128:H], head[:, H:]
        update = mtn(one[:, B:128], head)
        one[:, 128:H] = mm(one[:, 0:B], k13)
        two[...] = (
            psb[level, 0, :, 256:384] + psb[level, 1, :, 256:384] - jnp.where(lane < B, update[:, 128:], update[:, :128])
        )
        s23 = two[:, 0:B]
        tiles = gauss_jordan([[two[8 * i : 8 * i + 8, :]] for i in range(8)], B)
        corner = k33 - mtn(k13, one[:, 128:H])
        for i in range(8):
            two[8 * i : 8 * i + 8, :] = tiles[i][0]
        three[:, 0:B] = corner - mtn(s23, two[:, 0:B])

        pl.when(level == 0)(front)

        @pl.when(level != local)
        def _():
            upward(level, 2, left).wait_recv()

        lane = lax.broadcasted_iota(jnp.int32, (H, 128), 1)
        e_first, e_second = eb[level, first], eb[level, second]
        tail_first, tail_second = e_first[:, 128:W], e_second[:, 128:W]
        outer_f = [tail_first, tail_second]
        tail_first = jnp.where(lane == B, tail_first + tail_second, jnp.where(lane < B, tail_first, 0.0))
        e = jnp.concatenate([e_second, e_first[:, 0:128], tail_first], axis=1)
        m1 = mtn(one[:, 0:H], e[0:B])
        t2 = e[B:128] - m1[B:128]
        m2 = mtn(two[...], t2)
        tt[0:B] = e[0:B]
        tt[B:128] = t2
        tt[128:H] = e[128:H] - m1[128:H] - m2[0:B]
        gg[0:B] = m1[0:B]
        gg[B:128] = m2[B:128]
        low = gauss_jordan([[three[8 * i : 8 * i + 8, :]] for i in range(8)], 0)
        for i in range(8):
            three[8 * i : 8 * i + 8, :] = low[i][0]

        @pl.when(jnp.logical_and(level != local, level != merges))
        def _():
            upward(level, 3, left).wait_recv()

        gg[128:H] = mm(three[:, 0:B], tt[128:H])
        parts = packed(mtn(tt[:, 0:H], gg[:, 0:H]))
        for l in range(3):
            lanes = pl.ds(128 * l, 128)
            psb[level + 1, 0, :, lanes] = oob[level, second, :, lanes] - parts[l]

        send = jnp.logical_and(level < merges, level + 1 != local)

        @pl.when(send)
        def _():
            upward(level + 1, 0, above).start()
            upward(level + 1, 1, above).start()

        cross = mtn(tt[:, 0:H], gg[:, W:])
        eb[level + 1, 0, :, 0:128] = -cross[:, 0:128]
        outer = mtn(tt[:, W : W + H], gg[:, W:])
        shared_f = pltpu.roll(outer_f[1], 127, 1) - cross[:, 128:W]
        outer_f = outer_f[0] - pltpu.roll(outer[:, 128:W], 1, 1)
        eb[level + 1, 0, :, 128:W] = jnp.where(
            lane < B, -cross[:, 128:W], jnp.where(lane == B, shared_f, jnp.where(lane == B + 1, outer_f, 0.0))
        )

        @pl.when(send)
        def _():
            upward(level + 1, 2, above).start()

        parts = packed(outer)
        for l in range(3):
            lanes = pl.ds(128 * l, 128)
            oob[level + 1, 0, :, lanes] = oob[level, first, :, lanes] - parts[l]

        @pl.when(jnp.logical_and(send, level + 1 != merges))
        def _():
            upward(level + 1, 3, above).start()

        x3 = gg[128:H]
        x2 = gg[B:128] - mm(two[:, 0:B], x3)
        x1 = gg[0:B] - mm(one[:, B:128], x2) - mm(one[:, 128:H], x3)
        for r, x in enumerate((x1, x2, x3)):
            high, low = halves(x)
            xh[level, B * r : B * r + B] = high
            xl[level, B * r : B * r + B] = low
        return carry

    lane8 = lax.broadcasted_iota(jnp.int32, (8, W), 1)

    def descend(i, carry):
        level = merges - i
        first = first_slot(level)
        x = [jnp.where(lane8 < H, -xv[level + 1, q], jnp.where(lane8 == H, 1.0 - q, 0.0)) for q in (1, 0)]
        high, low = halves(jnp.concatenate(x, axis=1))
        y = mnt_narrow(high, xh[level]) + (mnt_narrow(low, xh[level]) + mnt_narrow(high, xl[level]))
        xv[level, 0] = xv[level + 1, first]
        xv[level, 1, :, 0:H] = y
        return carry

    def wait_up(level, carry):
        @pl.when(level != local)
        def _():
            for which in range(3):
                upward(level, which, left).wait_send()

        @pl.when(jnp.logical_and(level != local, level != merges))
        def _():
            upward(level, 3, left).wait_send()

        return carry

    @pl.when(i_bank == 0)
    def _():
        lax.fori_loop(0, merges + 1, ascend, 0)
        xv[...] = jnp.zeros_like(xv)
        lax.fori_loop(0, merges + 1, descend, 0)
        xout[0, 0] = xv[1, 1 - first_slot(0)]
        xout[0, 1] = xv[0, 1]
        downward().start()
        out_ref[:, 0:H] = xv[0, 0, 0:1, 0:H]
        out_ref[:, H:] = xv[0, 1, 0:1, 0:H]
        lax.fori_loop(1, merges + 1, wait_up, 0)
        downward().wait_send()

    @pl.when(i_bank == 1)
    def _():
        for which in range(4):
            upward(0, which, left).wait_send()
        downward().wait_recv()
        out_ref[:, 0:H] = xout[1, 0, 0:1, 0:H]
        out_ref[:, H:] = xout[1, 1, 0:1, 0:H]

    pl.when(has_above)(lambda: halo(0).wait_send())
    pl.when(has_below)(lambda: halo(1).wait_send())
    halo(2).wait_send()
    halo(3).wait_send()


def solve_tree(sizes, state, source, rate, jac, lift, sep, leaf):
    total = sizes[0] * sizes[1] * sizes[2]
    slots = total.bit_length() + 1
    channels, rows, cells = state.shape
    vmem, hbm = pl.BlockSpec(memory_space=pltpu.VMEM), pl.BlockSpec(memory_space=pltpu.HBM)
    return pl.pallas_call(
        functools.partial(tree_kernel, sizes),
        out_shape=jax.ShapeDtypeStruct((1, 2 * H), F32),
        in_specs=[hbm] * 5 + [vmem, hbm],
        out_specs=vmem,
        scratch_shapes=[
            *(pltpu.VMEM(x.shape, F32) for x in (state, source, rate, jac, lift, leaf)),
            pltpu.SemaphoreType.DMA((6,)),
            pltpu.VMEM((slots, 2, B, 2 * H), F32),
            pltpu.VMEM((slots, 2, H, W), F32),
            pltpu.VMEM((slots, 2, B, 2 * H), F32),
            pltpu.VMEM((B, H), F32),
            pltpu.VMEM((B, 128), F32),
            pltpu.VMEM((B, 128), F32),
            pltpu.VMEM((H, 2 * W), F32),
            pltpu.VMEM((H, 2 * W), F32),
            pltpu.VMEM((slots, H, 2 * W), BF16),
            pltpu.VMEM((slots, H, 2 * W), BF16),
            pltpu.VMEM((slots, 2, 8, W), F32),
            pltpu.VMEM((2, 2, 8, W), F32),
            pltpu.VMEM((2, channels, cells), F32),
            pltpu.VMEM((2, channels, cells), F32),
            pltpu.VMEM((2, channels, 128), F32),
            pltpu.VMEM((2, channels, 128), F32),
            pltpu.SemaphoreType.DMA((slots, 4)),
            pltpu.SemaphoreType.DMA((slots, 4)),
            pltpu.SemaphoreType.DMA((4,)),
            pltpu.SemaphoreType.DMA((4,)),
            pltpu.SemaphoreType.DMA,
            pltpu.SemaphoreType.DMA,
        ],
        compiler_params=pltpu.CompilerParams(
            collective_id=0, has_side_effects=True, vmem_limit_bytes=48 * 1024 * 1024
        ),
    )(*(pltpu.with_memory_space_constraint(x, pltpu.HBM) for x in (state, source, rate, jac, lift)), sep, pltpu.with_memory_space_constraint(leaf, pltpu.HBM))


def body(sizes, adjoint_state, adjoint_source, reaction_rate, jacobian, lifting, separator, leaf_schur):
    answer = solve_tree(
        sizes,
        adjoint_state[0],
        adjoint_source[0],
        reaction_rate[0],
        jacobian[0],
        lifting[0],
        separator.reshape(-1, 1),
        leaf_schur.reshape(2 * H, 2 * H),
    )
    return answer.reshape(1, 1, 1, 2 * H)


def solution(mesh):
    sizes = (mesh.shape["axial"], mesh.shape["azim"], mesh.shape["bank"])
    in_specs = (
        P("bank", None, "axial", "azim"),
        P("bank", None, "axial", "azim"),
        P("bank", "axial", "azim"),
        P("bank", None, None),
        P("bank", None, "axial", "azim"),
        P("axial", "azim", "bank", None),
        P("axial", "azim", "bank", None, None),
    )
    out_specs = P("axial", "azim", "bank", None)
    return jax.shard_map(
        functools.partial(body, sizes), mesh=mesh, in_specs=in_specs, out_specs=out_specs, check_vma=False
    )
```

```python
import functools

import jax
import jax.numpy as jnp
from jax import lax
from jax.experimental import pallas as pl
from jax.experimental.pallas import tpu as pltpu
from jax.sharding import PartitionSpec as P

highest = lax.Precision.HIGH
diffusion = 0.5
F32 = jnp.float32
BF16 = jnp.bfloat16
MESH = pl.DeviceIdType.MESH
H = 192
B = 64
W = 256


def mm(a, b):
    return lax.dot_general(a, b, (((1,), (0,)), ((), ())), precision=highest, preferred_element_type=F32)


def mtn(a, b):
    return lax.dot_general(a, b, (((0,), (0,)), ((), ())), precision=highest, preferred_element_type=F32)


def mnt(a, b):
    return lax.dot_general(a, b, (((1,), (1,)), ((), ())), precision=highest, preferred_element_type=F32)


def mnt_narrow(a, b):
    return lax.dot_general(a, b, (((1,), (1,)), ((), ())), preferred_element_type=F32)


def halves(x):
    high = x.astype(BF16)
    return high, (x - high.astype(F32)).astype(BF16)


def row_of(x, i):
    return jnp.broadcast_to(x[i : i + 1, :], x.shape)


def col_of(x, i):
    return jnp.take_along_axis(x, jnp.full(x.shape, i, jnp.int32), axis=1, mode="promise_in_bounds")


def tree_sum(terms):
    terms = list(terms)
    while len(terms) > 1:
        terms = [terms[i] + terms[i + 1] if i + 1 < len(terms) else terms[i] for i in range(0, len(terms), 2)]
    return terms[0]


def invert8(columns):
    sub = lax.broadcasted_iota(jnp.int32, (8, 128), 0)
    columns = list(columns)
    for p in range(0, 8, 2):
        x, y = columns[p], columns[p + 1]
        a, b, c = row_of(x, p), row_of(y, p), row_of(y, p + 1)
        scale = 1.0 / (a * c - b * b)
        first, second = sub == p, sub == p + 1
        pivot_rows = jnp.logical_or(first, second)
        hu = jnp.where(first, c, jnp.where(second, -b, y * b - x * c))
        hv = jnp.where(first, -b, jnp.where(second, a, x * b - y * a))
        for j in range(8):
            if j in (p, p + 1):
                continue
            u, v = row_of(columns[j], p), row_of(columns[j], p + 1)
            columns[j] = jnp.where(pivot_rows, 0.0, columns[j]) + (hu * u + hv * v) * scale
        columns[p] = hu * scale
        columns[p + 1] = hv * scale
    return columns


def gauss_jordan(tiles, offset):
    count, parts = len(tiles), len(tiles[0])
    sub = lax.broadcasted_iota(jnp.int32, (8, 128), 0)
    lane = lax.broadcasted_iota(jnp.int32, (8, 128), 1)

    def times(columns, rows):
        return tree_sum([c * r for c, r in zip(columns, rows)])

    def spread(value):
        return [row_of(value, j) for j in range(8)]

    def columns_of(value, start):
        return [col_of(value, start + j) for j in range(8)]

    for p in range(0, count, 2):
        q = p + 1
        start = offset + 8 * p
        block = jnp.logical_and(lane >= start, lane < start + 16)
        c11, c12 = columns_of(tiles[p][0], start), columns_of(tiles[p][0], start + 8)
        c21, c22 = columns_of(tiles[q][0], start), columns_of(tiles[q][0], start + 8)
        i1 = invert8(c11)
        y = [times(i1, spread(c12[j])) for j in range(8)]
        corner = [c22[j] - times(c21, spread(y[j])) for j in range(8)]
        upper, lower = list(tiles[p]), list(tiles[q])
        upper[0] = jnp.where(block, jnp.where(lane - start == sub, 1.0, 0.0), upper[0])
        lower[0] = jnp.where(block, jnp.where(lane - start - 8 == sub, 1.0, 0.0), lower[0])
        upper = [times(i1, spread(t)) for t in upper]
        lower = [t - times(c21, spread(u)) for t, u in zip(lower, upper)]
        i2 = invert8(corner)
        lower = [times(i2, spread(t)) for t in lower]
        lower_rows = [spread(t) for t in lower]
        upper = [u - times(y, rows) for u, rows in zip(upper, lower_rows)]
        upper_rows = [spread(t) for t in upper]
        for i in [i % count for i in range(q + 1, p + count)]:
            factors = columns_of(tiles[i][0], start) + columns_of(tiles[i][0], start + 8)
            fresh = []
            for l in range(parts):
                base = tiles[i][l]
                if l == 0:
                    base = jnp.where(block, 0.0, base)
                fresh.append(base - times(factors, upper_rows[l] + lower_rows[l]))
            tiles[i] = fresh
        tiles[p], tiles[q] = upper, lower
    return tiles


def packed(m):
    return [
        m[0:B, 0:128],
        jnp.concatenate([m[0:B, 128:H], m[128:H, 128:H]], axis=1),
        jnp.concatenate([m[B:128, 128:H], m[B:128, B:128]], axis=1),
    ]


def tree_kernel(
    sizes, state_in, source_in, rate_in, jac_in, lift_in, sep, leaf_in, out_ref,
    state, source, rate, jac, lift, leaf, in_sem,
    psb, eb, oob, one, two, three, tt, gg, xh, xl, xv, xout, edge_rows, halo_rows, edge_cols, halo_cols,
    up_send, up_recv, halo_send, halo_recv, down_send, down_recv,
):
    n_axial, n_azim, n_bank = sizes
    total = n_axial * n_azim * n_bank
    merges = total.bit_length() - 1
    local = merges - 1
    i_axial, i_azim, i_bank = lax.axis_index("axial"), lax.axis_index("azim"), lax.axis_index("bank")
    me = (i_axial * n_azim + i_azim) * n_bank + i_bank
    channels, rows_here, cells = state.shape

    def device(n):
        return (n // (n_azim * n_bank), (n // n_bank) % n_azim, n % n_bank)

    def field(level):
        bit = level if level < local else merges - 1
        azim_top = (n_bank * n_azim).bit_length() - 2
        if n_azim == 8 and bit == azim_top:
            return bit - 2, 3
        if n_axial == 32 and bit == azim_top + 3:
            return bit - 2, 3
        if n_axial == 32 and bit == azim_top + 5:
            return bit - 1, 2
        return bit, 1

    exchanges = [l for l in range(merges + 1) if l != local]

    def partner_at(level):
        low, width = field(level)
        value = (me // (1 << low)) % (1 << width)
        return me + ((1 << width) - 1 - 2 * value) * (1 << low)

    def partner(level):
        n = partner_at(0)
        for l in exchanges[1:]:
            n = jnp.where(level == l, partner_at(l), n)
        return n

    def first_slot(level):
        slot = jnp.int32(0)
        for l in range(merges + 1):
            bit = (me // (1 << l)) % 2
            here = 1 if l == local else (0 if l == merges else (1 - bit if l == merges - 2 else bit))
            slot = jnp.where(level == l, here, slot)
        return slot

    def piece(which, level, slot):
        if which == 0:
            return psb.at[level, slot, :, 0:128]
        if which == 1:
            return psb.at[level, slot, :, 128:384]
        return (eb if which == 2 else oob).at[level, slot]

    def upward(level, which, to):
        return pltpu.make_async_remote_copy(
            src_ref=piece(which, level, 0),
            dst_ref=piece(which, level, 1),
            send_sem=up_send.at[level, which],
            recv_sem=up_recv.at[level, which],
            device_id=to,
            device_id_type=MESH,
        )

    def downward():
        return pltpu.make_async_remote_copy(
            src_ref=xout.at[0],
            dst_ref=xout.at[1],
            send_sem=down_send,
            recv_sem=down_recv,
            device_id=device(partner_at(0)),
            device_id_type=MESH,
        )

    left = (i_axial, lax.rem(i_azim + n_azim - 1, n_azim), i_bank)
    right = (i_axial, lax.rem(i_azim + 1, n_azim), i_bank)
    above = (i_axial - 1, i_azim, i_bank)
    below = (i_axial + 1, i_azim, i_bank)
    has_above, has_below = i_axial > 0, i_axial < n_axial - 1

    def halo(which):
        src, dst, to = (
            (edge_rows.at[0], halo_rows.at[1], above),
            (edge_rows.at[1], halo_rows.at[0], below),
            (edge_cols.at[0], halo_cols.at[1], left),
            (edge_cols.at[1], halo_cols.at[0], right),
        )[which]
        return pltpu.make_async_remote_copy(
            src_ref=src,
            dst_ref=dst,
            send_sem=halo_send.at[which],
            recv_sem=halo_recv.at[which],
            device_id=to,
            device_id_type=MESH,
        )

    loads = [
        pltpu.make_async_copy(src, dst, in_sem.at[i])
        for i, (src, dst) in enumerate(
            ((leaf_in, leaf), (state_in, state), (source_in, source), (lift_in, lift), (rate_in, rate), (jac_in, jac))
        )
    ]
    for load in loads:
        load.start()
    halo_rows[...] = jnp.zeros_like(halo_rows)
    barrier = pltpu.get_barrier_semaphore()

    def greet(to):
        pl.semaphore_signal(barrier, inc=1, device_id=to, device_id_type=MESH)

    greet(left)
    greet(right)
    greet(device(partner_at(0)))
    pl.when(has_above)(lambda: greet(above))
    pl.when(has_below)(lambda: greet(below))

    @pl.when(i_bank == 0)
    def _():
        for level in exchanges[1:]:
            greet(device(partner_at(level)))

    loads[1].wait()
    lane128 = lax.broadcasted_iota(jnp.int32, (channels, 128), 1)
    edge_rows[0] = state[:, 0, :]
    edge_rows[1] = state[:, rows_here - 1, :]
    first_cols = jnp.zeros((channels, 128), F32)
    last_cols = jnp.zeros((channels, 128), F32)
    for r in range(rows_here):
        head, tail = state[:, r, 0:128], state[:, r, cells - 128 : cells]
        first_cols = jnp.where(lane128 == r, pltpu.roll(head, r, 1) if r else head, first_cols)
        last_cols = jnp.where(lane128 == r, pltpu.roll(tail, r + 1, 1), last_cols)
    edge_cols[0] = first_cols
    edge_cols[1] = last_cols

    def put(ref, level, parts):
        for l in range(3):
            ref[level, 0, :, 128 * l : 128 * l + 128] = parts[l]

    loads[0].wait()
    put(psb, 0, packed(leaf[H:, H:]))
    put(oob, 0, packed(leaf[:H, :H]))
    eb[0, 0, :, 0:H] = leaf[H:, :H]
    eb[0, 0, :, H:W] = jnp.zeros((H, W - H), F32)
    psb[local, 1] = jnp.zeros((B, 2 * H), F32)
    oob[local, 1] = jnp.zeros((B, 2 * H), F32)
    eb[local, 1] = jnp.zeros((H, W), F32)
    three[...] = jnp.zeros((B, 2 * B), F32)

    friends = 3 + jnp.where(has_above, 1, 0) + jnp.where(has_below, 1, 0)
    friends = friends + jnp.where(i_bank == 0, len(exchanges) - 1, 0)
    pl.semaphore_wait(barrier, friends)

    @pl.when(i_bank == 1)
    def _():
        for which in (0, 1, 3):
            upward(0, which, device(partner_at(0))).start()

    pl.when(has_above)(lambda: halo(0).start())
    pl.when(has_below)(lambda: halo(1).start())
    halo(2).start()
    halo(3).start()

    def front():
        pl.when(has_below)(lambda: halo(0).wait_recv())
        pl.when(has_above)(lambda: halo(1).wait_recv())
        halo(2).wait_recv()
        halo(3).wait_recv()
        for load in loads[2:]:
            load.wait()
        lane = lax.broadcasted_iota(jnp.int32, (channels, cells), 1)
        lane6 = lax.broadcasted_iota(jnp.int32, (sep.shape[0], cells), 1)
        jacobian = jac[...]
        rhs = jnp.zeros((channels, sep.shape[0]), F32)
        for r in range(rows_here):
            here = state[:, r, :]
            up = state[:, r - 1, :] if r else halo_rows[0]
            down = state[:, r + 1, :] if r < rows_here - 1 else halo_rows[1]
            before = jnp.where(lane == 0, halo_cols[0][:, r : r + 1], pltpu.roll(here, 1, 1))
            after = jnp.where(lane == cells - 1, halo_cols[1][:, r : r + 1], pltpu.roll(here, cells - 1, 1))
            reaction = mtn(jacobian, rate[r : r + 1, :] * here)
            residual = source[:, r, :] - reaction - diffusion * (4.0 * here - (up + down + before + after))
            picks = jnp.where(lane6 + r * cells == sep[...], 1.0, 0.0)
            rhs = rhs + mnt(residual, picks + lift[:, r, :])
        for c in range(3):
            eb[0, 0, c * channels : (c + 1) * channels, H : H + 1] = rhs[:, c + 3 : c + 4]
            eb[0, 0, c * channels : (c + 1) * channels, H + 1 : H + 2] = rhs[:, c : c + 1]

    @pl.when(i_bank == 1)
    def _():
        front()
        upward(0, 2, device(partner_at(0))).start()

    def ascend(level, carry):
        first = first_slot(level)
        second = 1 - first
        above = device(partner(level + 1))

        @pl.when(level != local)
        def _():
            upward(level, 0, left).wait_recv()

        def both(i):
            rows = pl.ds(8 * i, 8)
            return psb[level, 0, rows, 0:128] + psb[level, 1, rows, 0:128]

        tiles = gauss_jordan([[both(i)] for i in range(8)], 0)
        for i in range(8):
            one[8 * i : 8 * i + 8, 0:128] = tiles[i][0]

        @pl.when(level != local)
        def _():
            upward(level, 1, left).wait_recv()

        lane = lax.broadcasted_iota(jnp.int32, (B, 128), 1)
        head = psb[level, 0, :, 0:256] + psb[level, 1, :, 0:256]
        k13, k33 = head[:, 128:H], head[:, H:]
        update = mtn(one[:, B:128], head)
        one[:, 128:H] = mm(one[:, 0:B], k13)
        two[...] = (
            psb[level, 0, :, 256:384] + psb[level, 1, :, 256:384] - jnp.where(lane < B, update[:, 128:], update[:, :128])
        )
        s23 = two[:, 0:B]
        tiles = gauss_jordan([[two[8 * i : 8 * i + 8, :]] for i in range(8)], B)
        corner = k33 - mtn(k13, one[:, 128:H])
        for i in range(8):
            two[8 * i : 8 * i + 8, :] = tiles[i][0]
        three[:, 0:B] = corner - mtn(s23, two[:, 0:B])

        pl.when(level == 0)(front)

        @pl.when(level != local)
        def _():
            upward(level, 2, left).wait_recv()

        lane = lax.broadcasted_iota(jnp.int32, (H, 128), 1)
        e_first, e_second = eb[level, first], eb[level, second]
        tail_first, tail_second = e_first[:, 128:W], e_second[:, 128:W]
        outer_f = [tail_first, tail_second]
        tail_first = jnp.where(lane == B, tail_first + tail_second, jnp.where(lane < B, tail_first, 0.0))
        e = jnp.concatenate([e_second, e_first[:, 0:128], tail_first], axis=1)
        m1 = mtn(one[:, 0:H], e[0:B])
        t2 = e[B:128] - m1[B:128]
        m2 = mtn(two[...], t2)
        tt[0:B] = e[0:B]
        tt[B:128] = t2
        tt[128:H] = e[128:H] - m1[128:H] - m2[0:B]
        gg[0:B] = m1[0:B]
        gg[B:128] = m2[B:128]
        low = gauss_jordan([[three[8 * i : 8 * i + 8, :]] for i in range(8)], 0)
        for i in range(8):
            three[8 * i : 8 * i + 8, :] = low[i][0]

        gg[128:H] = mm(three[:, 0:B], tt[128:H])

        @pl.when(level < merges)
        def _():
            @pl.when(level != local)
            def _():
                upward(level, 3, left).wait_recv()

            parts = packed(mtn(tt[:, 0:H], gg[:, 0:H]))
            for l in range(3):
                lanes = pl.ds(128 * l, 128)
                psb[level + 1, 0, :, lanes] = oob[level, second, :, lanes] - parts[l]

            send = jnp.logical_and(level < merges, level + 1 != local)

            @pl.when(send)
            def _():
                upward(level + 1, 0, above).start()
                upward(level + 1, 1, above).start()

            cross = mtn(tt[:, 0:H], gg[:, W:])
            eb[level + 1, 0, :, 0:128] = -cross[:, 0:128]
            outer = mtn(tt[:, W : W + H], gg[:, W:])
            shared_f = pltpu.roll(outer_f[1], 127, 1) - cross[:, 128:W]
            own_f = outer_f[0] - pltpu.roll(outer[:, 128:W], 1, 1)
            eb[level + 1, 0, :, 128:W] = jnp.where(
                lane < B, -cross[:, 128:W], jnp.where(lane == B, shared_f, jnp.where(lane == B + 1, own_f, 0.0))
            )

            @pl.when(send)
            def _():
                upward(level + 1, 2, above).start()

            parts = packed(outer)
            for l in range(3):
                lanes = pl.ds(128 * l, 128)
                oob[level + 1, 0, :, lanes] = oob[level, first, :, lanes] - parts[l]

            @pl.when(jnp.logical_and(send, level + 1 != merges))
            def _():
                upward(level + 1, 3, above).start()

        x3 = gg[128:H]
        x2 = gg[B:128] - mm(two[:, 0:B], x3)
        x1 = gg[0:B] - mm(one[:, B:128], x2) - mm(one[:, 128:H], x3)
        for r, x in enumerate((x1, x2, x3)):
            high, low = halves(x)
            xh[level, B * r : B * r + B] = high
            xl[level, B * r : B * r + B] = low
        return carry

    lane8 = lax.broadcasted_iota(jnp.int32, (8, W), 1)

    def descend(i, carry):
        level = merges - i
        first = first_slot(level)
        x = [jnp.where(lane8 < H, -xv[level + 1, q], jnp.where(lane8 == H, 1.0 - q, 0.0)) for q in (1, 0)]
        high, low = halves(jnp.concatenate(x, axis=1))
        y = mnt_narrow(high, xh[level]) + (mnt_narrow(low, xh[level]) + mnt_narrow(high, xl[level]))
        xv[level, 0] = xv[level + 1, first]
        xv[level, 1, :, 0:H] = y
        return carry

    def wait_up(level, carry):
        @pl.when(level != local)
        def _():
            for which in range(3):
                upward(level, which, left).wait_send()

        @pl.when(jnp.logical_and(level != local, level != merges))
        def _():
            upward(level, 3, left).wait_send()

        return carry

    @pl.when(i_bank == 0)
    def _():
        lax.fori_loop(0, merges + 1, ascend, 0)
        xv[...] = jnp.zeros_like(xv)
        lax.fori_loop(0, merges + 1, descend, 0)
        xout[0, 0] = xv[1, 1 - first_slot(0)]
        xout[0, 1] = xv[0, 1]
        downward().start()
        out_ref[:, 0:H] = xv[0, 0, 0:1, 0:H]
        out_ref[:, H:] = xv[0, 1, 0:1, 0:H]
        lax.fori_loop(1, merges + 1, wait_up, 0)
        downward().wait_send()

    @pl.when(i_bank == 1)
    def _():
        for which in range(4):
            upward(0, which, left).wait_send()
        downward().wait_recv()
        out_ref[:, 0:H] = xout[1, 0, 0:1, 0:H]
        out_ref[:, H:] = xout[1, 1, 0:1, 0:H]

    pl.when(has_above)(lambda: halo(0).wait_send())
    pl.when(has_below)(lambda: halo(1).wait_send())
    halo(2).wait_send()
    halo(3).wait_send()


def solve_tree(sizes, state, source, rate, jac, lift, sep, leaf):
    total = sizes[0] * sizes[1] * sizes[2]
    slots = total.bit_length() + 1
    channels, rows, cells = state.shape
    vmem, hbm = pl.BlockSpec(memory_space=pltpu.VMEM), pl.BlockSpec(memory_space=pltpu.HBM)
    return pl.pallas_call(
        functools.partial(tree_kernel, sizes),
        out_shape=jax.ShapeDtypeStruct((1, 2 * H), F32),
        in_specs=[hbm] * 5 + [vmem, hbm],
        out_specs=vmem,
        scratch_shapes=[
            *(pltpu.VMEM(x.shape, F32) for x in (state, source, rate, jac, lift, leaf)),
            pltpu.SemaphoreType.DMA((6,)),
            pltpu.VMEM((slots, 2, B, 2 * H), F32),
            pltpu.VMEM((slots, 2, H, W), F32),
            pltpu.VMEM((slots, 2, B, 2 * H), F32),
            pltpu.VMEM((B, H), F32),
            pltpu.VMEM((B, 128), F32),
            pltpu.VMEM((B, 128), F32),
            pltpu.VMEM((H, 2 * W), F32),
            pltpu.VMEM((H, 2 * W), F32),
            pltpu.VMEM((slots, H, 2 * W), BF16),
            pltpu.VMEM((slots, H, 2 * W), BF16),
            pltpu.VMEM((slots, 2, 8, W), F32),
            pltpu.VMEM((2, 2, 8, W), F32),
            pltpu.VMEM((2, channels, cells), F32),
            pltpu.VMEM((2, channels, cells), F32),
            pltpu.VMEM((2, channels, 128), F32),
            pltpu.VMEM((2, channels, 128), F32),
            pltpu.SemaphoreType.DMA((slots, 4)),
            pltpu.SemaphoreType.DMA((slots, 4)),
            pltpu.SemaphoreType.DMA((4,)),
            pltpu.SemaphoreType.DMA((4,)),
            pltpu.SemaphoreType.DMA,
            pltpu.SemaphoreType.DMA,
        ],
        compiler_params=pltpu.CompilerParams(
            collective_id=0, has_side_effects=True, vmem_limit_bytes=48 * 1024 * 1024
        ),
    )(*(pltpu.with_memory_space_constraint(x, pltpu.HBM) for x in (state, source, rate, jac, lift)), sep, pltpu.with_memory_space_constraint(leaf, pltpu.HBM))


def body(sizes, adjoint_state, adjoint_source, reaction_rate, jacobian, lifting, separator, leaf_schur):
    answer = solve_tree(
        sizes,
        adjoint_state[0],
        adjoint_source[0],
        reaction_rate[0],
        jacobian[0],
        lifting[0],
        separator.reshape(-1, 1),
        leaf_schur.reshape(2 * H, 2 * H),
    )
    return answer.reshape(1, 1, 1, 2 * H)


def solution(mesh):
    sizes = (mesh.shape["axial"], mesh.shape["azim"], mesh.shape["bank"])
    in_specs = (
        P("bank", None, "axial", "azim"),
        P("bank", None, "axial", "azim"),
        P("bank", "axial", "azim"),
        P("bank", None, None),
        P("bank", None, "axial", "azim"),
        P("axial", "azim", "bank", None),
        P("axial", "azim", "bank", None, None),
    )
    out_specs = P("axial", "azim", "bank", None)
    return jax.shard_map(
        functools.partial(body, sizes), mesh=mesh, in_specs=in_specs, out_specs=out_specs, check_vma=False
    )
```
